32 devices in a mesh: crop: 4 (over z), scene: 8 (over y, x, core).
Axes of the slice: x: 2, y: 2, z: 4, core: 2. Of those that a mesh axis runs over, the one named last changes fastest.
Arguments:
- fine_feats: bfloat16 [4, 49152, 128], P('crop', 'scene'), may hold values from -6 to 6
- out_grad: bfloat16 [4, 49152, 128], P('crop', 'scene'), may hold values from -6 to 6
- pre_act: bfloat16 [4, 8, 8, 8, 64, 256], P('crop', 'scene'), may hold values from -6 to 6
- deep_grad: bfloat16 [4, 8, 8, 8, 64, 256], P('crop', 'scene'), may hold values from -6 to 6
- down_weight: bfloat16 [8, 128, 256], replicated, may hold values from -0.3125 to 0.3125
- up_weight: bfloat16 [8, 256, 128], replicated, may hold values from -0.375 to 0.375
- block_owner: int32 [4, 256, 1], P('crop', 'scene'), may hold values from 0 to 7; in each aligned block of 32 rows (0 to 31, 32 to 63, ..., all dimensions but the last counted through in order) at most 8 rows name the same one
- parent_slot: int32 [4, 49152], P('crop', 'scene'), may hold values from 0 to 63, as said below
- child_offset: int32 [4, 49152], P('crop', 'scene'), may hold values from 0 to 7, as said below
Outputs:
- fine_grad: bfloat16 [4, 49152, 128], P('crop', 'scene')
- down_grad: float32 [8, 128, 256], replicated
- up_grad: float32 [8, 256, 128], replicated
- bias_grad: float32 [256], replicated
The draws below stay inside these ranges and needn't reach their ends.
Inputs may be any that keep to these rules, and one draw needn't show every extreme that they name: `parent_slot`: within each aligned block of 192 fine sites the parent index never falls and each of the 64 parents has 1 to 8 sites. `child_offset`: offsets strictly rise within one parent. `block_owner`: among the 32 blocks of one scene index no owner is named more than 8 times, a bound that some block reaches.
All inputs are finite; a program needn't handle non-finite values.
Results may differ from the reference program's by a relative error of at most 0.005.
Values may be sent and summed in bfloat16 or wider, within the bound.
No kernel may reach another device: no remote copies, remote signals or barrier semaphores. Data moves between devices by JAX's collectives and lax.ppermute only.
A program may use at most 128 MiB of HBM per device.

```python
import math
import jax
import jax.numpy as jnp
import numpy as np
from jax import lax

C_IN = 128
C_OUT = 256
PB = 64
BR = 192
K = 32
CAPB = 8
BLOCKS = 256
FINE = 49152
CROPS = 4
N_SCENE = 8


def child_layout(key):
    block_keys = jax.random.split(jax.random.fold_in(key, 11), CROPS * BLOCKS)

    def one_block(block_key):
        first_key, second_key = jax.random.split(block_key)
        shuffled = jax.random.permutation(first_key, 7 * PB)
        extra = (shuffled < BR - PB).astype(jnp.int32).reshape(PB, 7).sum(axis=1)
        counts = 1 + extra
        scores = jax.random.randint(second_key, (PB, 8), 0, 1 << 20) * 8 + jnp.arange(8, dtype=jnp.int32)[None, :]
        ranks = jnp.argsort(jnp.argsort(scores, axis=1), axis=1)
        chosen = (ranks < counts[:, None]).astype(jnp.int32).reshape(-1)
        position = jnp.cumsum(chosen) - 1
        target = jnp.where(chosen > 0, position, BR)
        identity = jnp.arange(PB * 8, dtype=jnp.int32)
        slot_ids = jnp.zeros((BR,), jnp.int32).at[target].set(identity, mode='drop')
        return (slot_ids // 8, slot_ids % 8)
    parents, offsets = jax.vmap(one_block)(block_keys)
    return (parents.reshape(CROPS, BLOCKS * BR), offsets.reshape(CROPS, BLOCKS * BR))


def draw_parent_slot(key, part):
    return child_layout(key)[0]


def draw_child_offset(key, part):
    return child_layout(key)[1]


def levels(rng, shape, cuts, smallest, top_value):
    def one(axis_at, parts):
        draws = jax.random.uniform(jax.random.fold_in(jax.random.fold_in(rng, 6), axis_at), (parts,), jnp.float32, smallest / len(cuts), top_value / len(cuts))
        return jnp.repeat(jnp.exp(draws), shape[axis_at] // parts).reshape((-1,) + (1,) * (len(shape) - axis_at - 1))

    level = one(*cuts[0])
    for cut in cuts[1:]:
        level = level * one(*cut)
    return level


def shared_out(key, own, number, rows, count, top, reach, lean):
    order = jax.random.permutation(key, count)
    crowded, common = load_shares(count, rows * top, reach, lean, True), load_shares(count, rows * top, reach, lean, False)
    places = jnp.arange(count)

    def named(sizes, rotation):
        used = int((sizes > 0).sum())
        fixed = max(1, used // 4)
        shifted = fixed + (places - fixed + rotation * (used - fixed)) % max(1, count - fixed)
        return jnp.zeros((count,), jnp.int32).at[order[jnp.where(places < fixed, places, shifted)]].set(jnp.asarray(sizes, jnp.int32))

    sizes = jnp.where(number % 4 == 0, named(crowded, number // 4), named(common, number - number // 4 - 1))
    mixed = jax.random.permutation(jax.random.fold_in(own, 3), count)
    donor, taker = mixed[0:count // 2 * 2:2], mixed[1:count // 2 * 2:2]
    margin = jnp.minimum(sizes[donor] - 1, reach - sizes[taker]) // 2
    margin = jnp.where((donor == order[0]) | (taker == order[0]) | (sizes[taker] == 0), 0, jnp.maximum(margin, 0))
    shifted = jax.random.randint(jax.random.fold_in(own, 4), (count // 2,), 0, 1 << 20) % (margin + 1)
    sizes = sizes.at[donor].add(-shifted).at[taker].add(shifted)
    members = jnp.searchsorted(jnp.cumsum(sizes), jnp.arange(rows * top), side="right").astype(jnp.int32)
    listing = members.reshape(top, rows).T
    listing = listing[jax.random.permutation(jax.random.fold_in(own, 1), rows)]
    rotation = jax.random.randint(jax.random.fold_in(own, 2), (rows, 1), 0, top)
    return jnp.take_along_axis(listing, (jnp.arange(top)[None, :] + rotation) % top, axis=1)


def load_shares(amount, total, most, skew, full):
    loads = [(1 << 20) // math.isqrt(grade ** skew) + 1 for grade in range(1, amount + 1)]
    largest = most if full else min(most, max(-(-total // amount), total * loads[0] // sum(loads)))
    least = 1 if total - largest >= amount - 1 else 0
    given, rest = [largest] + [least] * (amount - 1), total - largest - least * (amount - 1)
    while rest > 0:
        free = [i for i in range(1, amount) if given[i] < largest] or [i for i in range(1, amount) if given[i] < most]
        mass, budget = sum([loads[i] for i in free]), rest
        for i in free:
            addition = min(most - given[i], max(1, budget * loads[i] // mass), rest)
            given[i] = given[i] + addition
            rest = rest - addition
    return np.array(given)


def noise(rng, shape, deviation, reach, cuts=(), kind=jnp.bfloat16):
    drawn = deviation * jax.random.normal(rng, shape, jnp.float32)
    if cuts:
        drawn = drawn * levels(rng, shape, cuts, -0.22, 0.18)
    return jnp.clip(drawn, -reach, reach).astype(kind)


def setup_inputs(seed: int = 0) -> dict:
    key_of = jax.random.split(jax.random.key(seed), 10)
    fine_feats = noise(key_of[0], (CROPS, FINE, C_IN), 1.0, 6.0, ((0, 4), (1, 8)))
    out_grad = noise(key_of[1], (CROPS, FINE, C_IN), 1.0, 6.0, ((0, 4), (1, 8)))
    pre_act = noise(key_of[2], (CROPS, N_SCENE, N_SCENE, CAPB, PB, C_OUT), 1.0, 6.0, ((0, 4), (1, 8)))
    deep_grad = noise(key_of[3], (CROPS, N_SCENE, N_SCENE, CAPB, PB, C_OUT), 1.0, 6.0, ((0, 4), (1, 8)))
    down_weight = noise(key_of[4], (8, C_IN, C_OUT), (3 * C_IN) ** -0.5, 0.3125)
    up_weight = noise(key_of[5], (8, C_OUT, C_IN), C_OUT ** -0.5, 0.375)
    block_owner_keys = jax.random.split(jax.random.fold_in(key_of[6], 1), CROPS * BLOCKS // K)
    block_owner_turns = jax.random.permutation(jax.random.fold_in(key_of[6], 3), CROPS * BLOCKS // K)
    block_owner = jax.vmap(lambda own, number: shared_out(jax.random.fold_in(key_of[6], 2), own, number, K, N_SCENE, 1, CAPB, 2))(block_owner_keys, block_owner_turns).reshape((CROPS, BLOCKS, 1))
    parent_slot = draw_parent_slot(jax.random.fold_in(key_of[9], 71), 0)
    child_offset = draw_child_offset(jax.random.fold_in(key_of[9], 71), 0)
    return {"fine_feats": fine_feats, "out_grad": out_grad, "pre_act": pre_act, "deep_grad": deep_grad, "down_weight": down_weight, "up_weight": up_weight, "block_owner": block_owner, "parent_slot": parent_slot, "child_offset": child_offset}


def silu_parts(pre_value):
    pre_float = pre_value.astype(jnp.float32)
    sig_value = jax.nn.sigmoid(pre_float)
    return pre_float * sig_value, sig_value * (1.0 + pre_float * (1.0 - sig_value))


def reference(fine_feats, out_grad, pre_act, deep_grad, down_weight, up_weight, block_owner, parent_slot, child_offset):
    wu_mat = jnp.transpose(up_weight, (0, 2, 1)).reshape(8 * C_IN, C_OUT)
    wd_mat = jnp.transpose(down_weight, (2, 0, 1)).reshape(C_OUT, 8 * C_IN)
    earlier = jnp.arange(K)[None, :] < jnp.arange(K)[:, None]
    places = (parent_slot * 8 + child_offset).astype(jnp.int32)
    block_base = jnp.repeat(jnp.arange(K, dtype=jnp.int32) * (PB * 8), BR)
    up_sum = jnp.zeros((C_OUT, 8 * C_IN), jnp.float32)
    down_sum = jnp.zeros((8 * C_IN, C_OUT), jnp.float32)
    bias_sum = jnp.zeros((C_OUT,), jnp.float32)
    results = []
    for crop_index in range(CROPS):
        owners = block_owner[crop_index, :, 0].reshape(N_SCENE, K)
        same_owner = owners[:, :, None] == owners[:, None, :]
        slot_rank = jnp.sum(same_owner & earlier[None], axis=2).astype(jnp.int32)
        pre_crop = pre_act[crop_index]
        deep_crop = deep_grad[crop_index]

        def block_step(totals, inputs):
            up_acc, down_acc, bias_acc = totals
            source, owner_row, rank_row, feats, cotan, place_row = inputs
            parent_pre = pre_crop[owner_row, source, rank_row].reshape(K * PB, C_OUT)
            parent_deep = deep_crop[owner_row, source, rank_row].reshape(K * PB, C_OUT)
            flat_index = (block_base + place_row).astype(jnp.int32)
            feat_slots = jnp.zeros((K * PB * 8, C_IN), fine_feats.dtype).at[flat_index].set(feats).reshape(K * PB, 8 * C_IN)
            cot_slots = jnp.zeros((K * PB * 8, C_IN), out_grad.dtype).at[flat_index].set(cotan).reshape(K * PB, 8 * C_IN)
            act_value, slope_value = silu_parts(parent_pre)
            act_grad = parent_deep.astype(jnp.float32) + jnp.dot(cot_slots, wu_mat, preferred_element_type=jnp.float32)
            pre_grad = (act_grad * slope_value).astype(jnp.bfloat16)
            slot_grads = jnp.dot(pre_grad, wd_mat, preferred_element_type=jnp.float32).reshape(K * PB * 8, C_IN)
            fine_part = slot_grads[flat_index].astype(jnp.bfloat16)
            up_acc = up_acc + jnp.dot(act_value.astype(jnp.bfloat16).T, cot_slots, preferred_element_type=jnp.float32)
            down_acc = down_acc + jnp.dot(feat_slots.T, pre_grad, preferred_element_type=jnp.float32)
            bias_acc = bias_acc + jnp.sum(pre_grad.astype(jnp.float32), axis=0)
            return (up_acc, down_acc, bias_acc), fine_part

        inputs = (jnp.arange(N_SCENE, dtype=jnp.int32), owners, slot_rank,
                  fine_feats[crop_index].reshape(N_SCENE, K * BR, C_IN),
                  out_grad[crop_index].reshape(N_SCENE, K * BR, C_IN),
                  places[crop_index].reshape(N_SCENE, K * BR))
        (up_sum, down_sum, bias_sum), fine_all = lax.scan(block_step, (up_sum, down_sum, bias_sum), inputs)
        results.append(fine_all.reshape(FINE, C_IN))
    grad_scale = float(CROPS * FINE) ** -0.5
    up_grad = jnp.transpose((up_sum * grad_scale).reshape(C_OUT, 8, C_IN), (1, 0, 2))
    down_grad = (down_sum * grad_scale).reshape(8, C_IN, C_OUT)
    return jnp.stack(results), down_grad, up_grad, bias_sum * grad_scale
```

```python
import jax
import jax.numpy as jnp
from jax import lax
from jax.experimental import pallas as pl
from jax.experimental.pallas import tpu as pltpu
from jax.sharding import PartitionSpec as P


F32 = jnp.float32
BF16 = jnp.bfloat16
NT = (((1,), (1,)), ((), ()))
TN = (((0,), (0,)), ((), ()))
BIAS_ROWS = 16


def swap(value, axis, step):
    size = lax.axis_size(axis)
    return lax.ppermute(value, axis, [(i, i ^ step) for i in range(size)])


def expand_kernel(places, feats, cotan, up_weight, feat_slots, cot_slots, conv, wide):
    group = places.shape[1]
    rows, width = feats.shape[0] // group, feats.shape[1]
    parents = feat_slots.shape[0] // group

    @pl.when(pl.program_id(0) == 0)
    def _():
        for k in range(8):
            wide[:, k * width : (k + 1) * width] = up_weight[k]

    for i in range(group):
        place = places[0, i : i + 1, :]
        slots = lax.broadcasted_iota(jnp.int32, (parents * 8, rows), 0)
        chooser = jnp.where(slots == place, 1.0, 0.0).astype(BF16)
        both = jnp.concatenate(
            [feats[i * rows : (i + 1) * rows, :], cotan[i * rows : (i + 1) * rows, :]], axis=1
        )
        spread = jnp.dot(chooser, both, preferred_element_type=F32).astype(BF16)
        for k in range(8):
            to = (slice(i * parents, (i + 1) * parents), slice(k * width, (k + 1) * width))
            feat_slots[to] = spread[k * parents : (k + 1) * parents, :width]
            cot_slots[to] = spread[k * parents : (k + 1) * parents, width:]
    conv[...] = lax.dot_general(cot_slots[...], wide[...], NT, preferred_element_type=F32)


def start_gather(table, me, whole, received, buffer, sems):
    capacity = whole.shape[1]
    for k in range(len(received) + 1):
        for j in range(capacity):
            block = table[k * capacity + j]

            @pl.when(block >= 0)
            def _():
                source = whole.at[me, j] if k == 0 else received[k - 1].at[j]
                pltpu.make_async_copy(source, buffer.at[block], sems.at[block]).start()


def wait_group(step, group, whole, buffer, sems):
    for i in range(group):
        block = step * group + i
        pltpu.make_async_copy(whole.at[0, 0], buffer.at[block], sems.at[block]).wait()


def deal(total, ids, mine, other, extra=None):
    pieces = 2 * mine.shape[0]
    width = mine.shape[2]
    per = pieces // 8
    rows = total.shape[0] // per
    for m in range(pieces):
        k, part = m // per, m % per
        tile = total[part * rows : (part + 1) * rows, k * width : (k + 1) * width]

        @pl.when(ids[1] == m % 2)
        def _():
            mine[m // 2, :rows, :] = tile
            if extra is not None:
                mine[m // 2, rows:, :] = extra

        @pl.when(ids[1] != m % 2)
        def _():
            other[m // 2, :rows, :] = tile.astype(BF16)
            if extra is not None:
                other[m // 2, rows:, :] = extra.astype(BF16)


def act_kernel(group, count, table, ids, whole, *refs):
    received, (cot_slots, slope, mine, other, buffer, total, sems) = refs[:count], refs[count:]
    step = pl.program_id(0)

    @pl.when(step == 0)
    def _():
        total[...] = jnp.zeros_like(total)
        start_gather(table, ids[0], whole, received, buffer, sems)

    wait_group(step, group, whole, buffer, sems)
    pre = buffer[pl.ds(step * group, group)].astype(F32).reshape(-1, buffer.shape[2])
    sig = jax.nn.sigmoid(pre)
    slope[...] = sig * (1.0 + pre * (1.0 - sig))
    act = (pre * sig).astype(BF16)
    total[...] += lax.dot_general(act, cot_slots[...], TN, preferred_element_type=F32)

    @pl.when(step == pl.num_programs(0) - 1)
    def _():
        deal(total, ids, mine, other)


def pre_kernel(group, count, table, ids, whole, *refs):
    received, rest = refs[:count], refs[count:]
    feat_slots, conv, slope, pre_grad, mine, other, buffer, total, bias, sems = rest
    step = pl.program_id(0)

    @pl.when(step == 0)
    def _():
        total[...] = jnp.zeros_like(total)
        bias[...] = jnp.zeros_like(bias)
        start_gather(table, ids[0], whole, received, buffer, sems)

    wait_group(step, group, whole, buffer, sems)
    deep = buffer[pl.ds(step * group, group)].astype(F32).reshape(-1, buffer.shape[2])
    grad = ((deep + conv[...]) * slope[...]).astype(BF16)
    pre_grad[...] = grad
    wide = grad.astype(F32)
    bias[...] += jnp.sum(wide.reshape(-1, 8, wide.shape[1]), axis=0)
    total[...] += lax.dot_general(grad, feat_slots[...], TN, preferred_element_type=F32)

    @pl.when(step == pl.num_programs(0) - 1)
    def _():
        width = mine.shape[2]
        line = jnp.sum(bias[...], axis=0, keepdims=True)
        halves = [line[:, i * width : (i + 1) * width] for i in range(line.shape[1] // width)]
        row = lax.broadcasted_iota(jnp.int32, (BIAS_ROWS, width), 0)
        extra = jnp.zeros((BIAS_ROWS, width), F32)
        for i, half in enumerate(halves):
            extra = jnp.where(row == i, half, extra)
        deal(total, ids, mine, other, extra)


def fine_kernel(places, pre_grad, down_weight, fine):
    group = places.shape[1]
    rows, width = fine.shape[0] // group, fine.shape[1]
    parents = pre_grad.shape[0] // group
    slot_grads = lax.dot_general(
        pre_grad[...], down_weight[...], NT, preferred_element_type=F32
    ).astype(BF16)
    for i in range(group):
        place = places[0, i : i + 1, :]
        slots = lax.broadcasted_iota(jnp.int32, (parents * 8, rows), 0)
        chooser = jnp.where(slots == place, 1.0, 0.0).astype(BF16)
        tall = jnp.concatenate(
            [
                slot_grads[i * parents : (i + 1) * parents, k * width : (k + 1) * width]
                for k in range(8)
            ],
            axis=0,
        )
        fine[i * rows : (i + 1) * rows, :] = lax.dot_general(
            chooser, tall, TN, preferred_element_type=F32
        ).astype(BF16)


def split_kernel(ids, mine, arrived, own, *sends):
    chip = ids[2]
    own[...] = mine[chip] + arrived[chip].astype(F32)
    for d, send in enumerate(sends):
        peer = chip ^ (d + 1)
        send[...] = (mine[peer] + arrived[peer].astype(F32)).astype(BF16)


def tree(values):
    while len(values) > 1:
        values = [values[i] + values[i + 1] for i in range(0, len(values), 2)]
    return values[0]


def sum_kernel(*refs):
    *parts, out = refs
    out[...] = tree([part[...].astype(F32) for part in parts]).astype(BF16)


def finish_kernel(scale, ids, *refs):
    pieces = (len(refs) - 3) // 2
    ups, downs = refs[:pieces], refs[pieces : 2 * pieces]
    up_grad, down_grad, bias_grad = refs[2 * pieces :]
    per = pieces // 8
    rows = ups[0].shape[0]
    me = ids[0]
    for i in range(pieces):
        m = me ^ i
        k, part = m // per, m % per
        up = ups[i][...].astype(F32) * scale
        down = jnp.transpose(downs[i][:rows, :].astype(F32) * scale)
        if per == 1:
            up_grad[m] = up
            down_grad[m] = down
        else:
            up_grad[k, pl.ds(pl.multiple_of(part * rows, rows), rows), :] = up
            for q in range(per):

                @pl.when(part == q)
                def _():
                    down_grad[k, :, q * rows : (q + 1) * rows] = down

        @pl.when(m == 0)
        def _():
            bias_grad[...] = downs[i][rows:, :].astype(F32)[:8] * scale


def whole_spec(shape):
    return pl.BlockSpec(shape, lambda *_: (0,) * len(shape))


def small_call(kernel, ids, inputs, outputs):
    spec = pltpu.PrefetchScalarGridSpec(
        num_scalar_prefetch=0 if ids is None else 1,
        grid=(1,),
        in_specs=[whole_spec(x.shape) for x in inputs],
        out_specs=[whole_spec(x.shape) for x in outputs],
    )
    call = pl.pallas_call(kernel, grid_spec=spec, out_shape=outputs)
    return call(*inputs) if ids is None else call(ids, *inputs)


def reduce_pieces(ids, mine, other):
    scene_count = lax.axis_size("scene")
    crop_count = lax.axis_size("crop")
    chips = scene_count // 2
    piece = jax.ShapeDtypeStruct(mine.shape[1:], BF16)
    arrived = swap(other, "scene", 1)
    own, *sends = small_call(
        split_kernel,
        ids,
        [mine, arrived],
        [jax.ShapeDtypeStruct(piece.shape, F32)] + [piece] * (chips - 1),
    )
    parts = [own] + [swap(send, "scene", 2 * (d + 1)) for d, send in enumerate(sends)]
    (part,) = small_call(sum_kernel, None, parts, [piece])
    parts = [part] + [swap(part, "crop", d) for d in range(1, crop_count)]
    (done,) = small_call(sum_kernel, None, parts, [piece])
    even = [done] + [swap(done, "scene", 2 * d) for d in range(1, chips)]
    odd = [swap(x, "scene", 1) for x in even]
    return [x for pair in zip(even, odd) for x in pair]


def exchange(array):
    me = lax.axis_index("scene")
    count = array.shape[0]
    order = [6, 2, 4, 7, 3, 5, 1] if count == 8 else list(range(1, count))
    out = {}
    for k in order:
        out[k] = swap(lax.dynamic_index_in_dim(array, me ^ k, 0, keepdims=False), "scene", k)
    return [out[k] for k in range(1, count)]


def on_device(
    fine_feats,
    out_grad,
    pre_act,
    deep_grad,
    down_weight,
    up_weight,
    block_owner,
    parent_slot,
    child_offset,
):
    scene_count = lax.axis_size("scene")
    crop_count = lax.axis_size("crop")
    width = fine_feats.shape[2]
    out_width = pre_act.shape[5]
    capacity = pre_act.shape[3]
    parents = pre_act.shape[4]
    owners = block_owner[0, :, 0]
    blocks = owners.shape[0]
    fine_rows = fine_feats.shape[1]
    rows = fine_rows // blocks
    group = 256 // parents
    steps = blocks // group
    slots = group * parents
    me = lax.axis_index("scene").astype(jnp.int32)
    ids = jnp.stack([me, me % 2, me // 2])

    pre_whole, deep_whole = pre_act[0, 0], deep_grad[0, 0]
    pre_received = exchange(pre_whole)
    deep_received = exchange(deep_whole)

    earlier = jnp.arange(blocks)[None, :] < jnp.arange(blocks)[:, None]
    same_owner = owners[:, None] == owners[None, :]
    slot_rank = jnp.sum(same_owner & earlier, axis=1).astype(jnp.int32)
    target = (owners ^ me) * capacity + slot_rank
    hit = target[None, :] == jnp.arange(scene_count * capacity, dtype=jnp.int32)[:, None]
    table = jnp.max(jnp.where(hit, jnp.arange(blocks, dtype=jnp.int32)[None, :], -1), axis=1)

    places = (child_offset[0] * parents + parent_slot[0]).reshape(steps, group, rows)
    place_spec = pl.BlockSpec((1, group, rows), lambda g, *_: (g, 0, 0))
    fine_spec = pl.BlockSpec((group * rows, width), lambda g, *_: (g, 0))
    slot_spec = pl.BlockSpec((slots, 8 * width), lambda g, *_: (g, 0))
    coarse_spec = pl.BlockSpec((slots, out_width), lambda g, *_: (g, 0))
    any_spec = pl.BlockSpec(memory_space=pl.ANY)
    total_rows = blocks * parents
    slot_shape = jax.ShapeDtypeStruct((total_rows, 8 * width), BF16)
    coarse_f32 = jax.ShapeDtypeStruct((total_rows, out_width), F32)

    feat_slots, cot_slots, conv = pl.pallas_call(
        expand_kernel,
        grid=(steps,),
        in_specs=[place_spec, fine_spec, fine_spec, whole_spec(up_weight.shape)],
        out_specs=[slot_spec, slot_spec, coarse_spec],
        out_shape=[slot_shape, slot_shape, coarse_f32],
        scratch_shapes=[pltpu.VMEM((out_width, 8 * width), BF16)],
    )(places, fine_feats[0], out_grad[0], up_weight)

    chips = scene_count // 2
    piece_rows = 8 * out_width // scene_count

    def dealt(extra):
        shape = (chips, piece_rows + extra, width)
        shapes = [jax.ShapeDtypeStruct(shape, F32), jax.ShapeDtypeStruct(shape, BF16)]
        return shapes, [whole_spec(shape)] * 2

    scratch = [
        pltpu.VMEM((blocks, parents, out_width), BF16),
        pltpu.VMEM((out_width, 8 * width), F32),
    ]
    shapes, specs = dealt(0)
    slope, up_mine, up_other = pl.pallas_call(
        lambda *refs: act_kernel(group, scene_count - 1, *refs),
        grid_spec=pltpu.PrefetchScalarGridSpec(
            num_scalar_prefetch=2,
            grid=(steps,),
            in_specs=[any_spec] * scene_count + [slot_spec],
            out_specs=[coarse_spec] + specs,
            scratch_shapes=scratch + [pltpu.SemaphoreType.DMA((blocks,))],
        ),
        out_shape=[coarse_f32] + shapes,
    )(table, ids, pre_whole, *pre_received, cot_slots)
    up_pieces = reduce_pieces(ids, up_mine, up_other)

    shapes, specs = dealt(BIAS_ROWS)
    pre_grad, down_mine, down_other = pl.pallas_call(
        lambda *refs: pre_kernel(group, scene_count - 1, *refs),
        grid_spec=pltpu.PrefetchScalarGridSpec(
            num_scalar_prefetch=2,
            grid=(steps,),
            in_specs=[any_spec] * scene_count + [slot_spec, coarse_spec, coarse_spec],
            out_specs=[coarse_spec] + specs,
            scratch_shapes=scratch
            + [pltpu.VMEM((8, out_width), F32), pltpu.SemaphoreType.DMA((blocks,))],
        ),
        out_shape=[jax.ShapeDtypeStruct((total_rows, out_width), BF16)] + shapes,
    )(table, ids, deep_whole, *deep_received, feat_slots, conv, slope)
    down_pieces = reduce_pieces(ids, down_mine, down_other)

    fine = pl.pallas_call(
        fine_kernel,
        grid=(steps,),
        in_specs=[place_spec, coarse_spec, whole_spec((8 * width, out_width))],
        out_specs=fine_spec,
        out_shape=jax.ShapeDtypeStruct((fine_rows, width), BF16),
    )(places, pre_grad, down_weight.reshape(8 * width, out_width))

    scale = float(crop_count * scene_count * fine_rows) ** (-0.5)
    up_grad, down_grad, bias_grad = small_call(
        lambda *refs: finish_kernel(scale, *refs),
        ids,
        up_pieces + down_pieces,
        [
            jax.ShapeDtypeStruct((8, out_width, width), F32),
            jax.ShapeDtypeStruct((8, width, out_width), F32),
            jax.ShapeDtypeStruct((8, width), F32),
        ],
    )
    bias = bias_grad[: out_width // width].reshape(out_width)
    return (fine[None], down_grad, up_grad, bias)


def solution(mesh):
    return jax.shard_map(
        on_device,
        mesh=mesh,
        in_specs=(
            P("crop", "scene", None),
            P("crop", "scene", None),
            P("crop", "scene", None, None, None, None),
            P("crop", "scene", None, None, None, None),
            P(),
            P(),
            P("crop", "scene", None),
            P("crop", "scene"),
            P("crop", "scene"),
        ),
        out_specs=(P("crop", "scene", None), P(), P(), P()),
        check_vma=False,
    )
```

```python
import jax
import jax.numpy as jnp
from jax import lax
from jax.experimental import pallas as pl
from jax.experimental.pallas import tpu as pltpu
from jax.sharding import PartitionSpec as P


F32 = jnp.float32
BF16 = jnp.bfloat16
NT = (((1,), (1,)), ((), ()))
TN = (((0,), (0,)), ((), ()))
BIAS_ROWS = 16
FINE_PARTS = 4


def swap(value, axis, step):
    size = lax.axis_size(axis)
    return lax.ppermute(value, axis, [(i, i ^ step) for i in range(size)])


def expand_kernel(places, feats, cotan, up_weight, feat_slots, cot_slots, conv, wide, slot_rows):
    step = pl.program_id(0)
    group = places.shape[1]
    rows, width = feats.shape[0] // group, feats.shape[1]
    parents = slot_rows.shape[0] // group
    slots = slot_rows.shape[0]

    @pl.when(step == 0)
    def _():
        for k in range(8):
            wide[:, k * width : (k + 1) * width] = up_weight[k]

    at = pl.ds(pl.multiple_of(step * slots, slots), slots)
    for i in range(group):
        place = places[0, i : i + 1, :]
        ids = lax.broadcasted_iota(jnp.int32, (parents * 8, rows), 0)
        chooser = jnp.where(ids == place, 1.0, 0.0).astype(BF16)
        both = jnp.concatenate(
            [feats[i * rows : (i + 1) * rows, :], cotan[i * rows : (i + 1) * rows, :]], axis=1
        )
        spread = jnp.dot(chooser, both, preferred_element_type=F32).astype(BF16)
        for k in range(8):
            to = (slice(i * parents, (i + 1) * parents), slice(k * width, (k + 1) * width))
            slot_rows[to] = spread[k * parents : (k + 1) * parents, :width]
            cot_slots[
                pl.ds(pl.multiple_of(step * slots + i * parents, parents), parents),
                k * width : (k + 1) * width,
            ] = spread[k * parents : (k + 1) * parents, width:]
    feat_slots[:, at] = jnp.transpose(slot_rows[...])
    conv[at, :] = lax.dot_general(cot_slots[at, :], wide[...], NT, preferred_element_type=F32)


def each_block(table, received, body):
    capacity = received[0].shape[0]
    for k, ref in enumerate(received):
        count = table[len(received) * capacity + k]

        def one(j, _, k=k, ref=ref):
            body(ref, j, table[k * capacity + j])

        lax.fori_loop(0, count, one, None)


def deal(tiles, ids, mine, other, extra=None):
    for m, tile in enumerate(tiles):
        rows = tile.shape[0]

        @pl.when(ids[1] == m % 2)
        def _():
            mine[m // 2, :rows, :] = tile
            if extra is not None:
                mine[m // 2, rows:, :] = extra

        @pl.when(ids[1] != m % 2)
        def _():
            other[m // 2, :rows, :] = tile.astype(BF16)
            if extra is not None:
                other[m // 2, rows:, :] = extra.astype(BF16)


def act_kernel(count, table, ids, *refs):
    received, (cot_slots, slope, mine, other, act, total) = refs[:count], refs[count:]
    parents = received[0].shape[1]

    def silu(ref, j, block):
        pre = ref[j].astype(F32)
        sig = 0.5 * jnp.tanh(0.5 * pre) + 0.5
        at = pl.ds(pl.multiple_of(block * parents, parents), parents)
        slope[at, :] = sig * (1.0 + pre * (1.0 - sig))
        act[at, :] = (pre * sig).astype(BF16)

    each_block(table, received, silu)
    total[...] = lax.dot_general(act[...], cot_slots[...], TN, preferred_element_type=F32)
    pieces, rows, width = 2 * mine.shape[0], mine.shape[1], mine.shape[2]
    per = pieces // 8
    tiles = [
        total[(m % per) * rows : (m % per + 1) * rows, m // per * width : (m // per + 1) * width]
        for m in range(pieces)
    ]
    deal(tiles, ids, mine, other)


def pre_kernel(count, table, ids, *refs):
    received, rest = refs[:count], refs[count:]
    feat_slots, conv, slope, pre_grad, mine, other, total, bias = rest
    bias[...] = jnp.zeros_like(bias)
    parents = received[0].shape[1]

    def one(ref, j, block):
        at = pl.ds(pl.multiple_of(block * parents, parents), parents)
        grad = ((ref[j].astype(F32) + conv[at, :]) * slope[at, :]).astype(BF16)
        pre_grad[at, :] = grad
        wide = grad.astype(F32)
        bias[...] += jnp.sum(wide.reshape(-1, 8, wide.shape[1]), axis=0)

    each_block(table, received, one)
    total[...] = jnp.dot(feat_slots[...], pre_grad[...], preferred_element_type=F32)
    pieces = 2 * mine.shape[0]
    rows = total.shape[0] // pieces
    tiles = [total[m * rows : (m + 1) * rows, :] for m in range(pieces)]
    line = jnp.sum(bias[...], axis=0, keepdims=True)
    row = lax.broadcasted_iota(jnp.int32, (BIAS_ROWS, line.shape[1]), 0)
    high = line.astype(BF16).astype(F32)
    extra = jnp.where(row == 0, high, jnp.where(row == 1, line - high, 0.0))
    deal(tiles, ids, mine, other, extra)


def fine_kernel(places, pre_grad, down_weight, *refs):
    fine = refs[-1]
    group = places.shape[2]
    rows, width = fine.shape[0] // group, fine.shape[1]
    parents = pre_grad.shape[0] // group
    slot_grads = lax.dot_general(
        pre_grad[...], down_weight[...], NT, preferred_element_type=F32
    ).astype(BF16)
    for i in range(group):
        slots = lax.broadcasted_iota(jnp.int32, (rows, parents * 8), 1)
        chooser = jnp.where(slots == places[0, :, i : i + 1], 1.0, 0.0).astype(BF16)
        tall = jnp.concatenate(
            [
                slot_grads[i * parents : (i + 1) * parents, k * width : (k + 1) * width]
                for k in range(8)
            ],
            axis=0,
        )
        fine[i * rows : (i + 1) * rows, :] = jnp.dot(
            chooser, tall, preferred_element_type=F32
        ).astype(BF16)


def tree(values):
    while len(values) > 1:
        values = [values[i] + values[i + 1] for i in range(0, len(values), 2)]
    return values[0]


def finish_kernel(scale, with_bias, ids, *refs):
    pieces = len(refs) - 1 - with_bias
    out = refs[pieces]
    for i in range(pieces):
        m = ids[0] ^ i
        rows = out.shape[1]
        out[m] = refs[i][:rows, :].astype(F32) * scale
        if with_bias:

            @pl.when(m == 0)
            def _():
                pair = refs[i][rows : rows + 8, :].astype(F32)
                refs[-1][...] = (pair[0:1] + pair[1:2]) * scale


def grant(mebibytes):
    return pltpu.CompilerParams(vmem_limit_bytes=mebibytes << 20)


def whole_spec(shape):
    return pl.BlockSpec(shape, lambda *_: (0,) * len(shape))


def finish(scale, ids, pieces, shape, with_bias):
    outputs = [jax.ShapeDtypeStruct(shape, F32)]
    if with_bias:
        outputs.append(jax.ShapeDtypeStruct((1, shape[2]), F32))
    return pl.pallas_call(
        lambda *refs: finish_kernel(scale, with_bias, *refs),
        grid_spec=pltpu.PrefetchScalarGridSpec(
            num_scalar_prefetch=1,
            grid=(1,),
            in_specs=[whole_spec(x.shape) for x in pieces],
            out_specs=[whole_spec(x.shape) for x in outputs],
        ),
        out_shape=outputs,
        compiler_params=grant(12),
    )(ids, *pieces)


def row_of(array, index):
    start = (index,) + (jnp.uint32(0),) * (array.ndim - 1)
    return lax.dynamic_slice(array, start, (1,) + array.shape[1:])[0]


def sum_plane(peers, mine, other):
    chips = mine.shape[0]
    arrived = swap(other, "scene", 1)

    def both(peer):
        return row_of(mine, peer) + row_of(arrived, peer).astype(F32)

    sends = {d: both(peers[d]).astype(BF16) for d in range(1, chips)}
    parts = {d: swap(sends[d], "scene", 2 * d) for d in far_first(chips)}
    return tree([both(peers[0])] + [parts[d].astype(F32) for d in range(1, chips)]).astype(BF16)


def far_first(count):
    return sorted(range(1, count), key=lambda d: -bin(d).count("1"))


def sum_crops(part):
    crops = lax.axis_size("crop")
    parts = {d: swap(part, "crop", d) for d in far_first(crops)}
    return tree([part.astype(F32)] + [parts[d].astype(F32) for d in range(1, crops)]).astype(BF16)


def spread(done):
    chips = lax.axis_size("scene") // 2
    even = {d: swap(done, "scene", 2 * d) for d in far_first(chips)}
    even[0] = done
    odd = {d: swap(even[d], "scene", 1) for d in range(chips)}
    return [x for d in range(chips) for x in (even[d], odd[d])]


def exchange(array, peers):
    count = array.shape[0]
    order = exchange_order(count)
    out = {}
    for group in (order[:2], order[2:] + [0]):
        sends = {k: row_of(array, peers[k]) for k in group}
        array, *held = lax.optimization_barrier((array, *sends.values()))
        for k, send in zip(group, held):
            out[k] = send if k == 0 else swap(send, "scene", k)
    return [out[k] for k in range(count)]


def exchange_order(count):
    return [6, 2, 4, 7, 3, 5, 1] if count == 8 else list(range(1, count))


def on_device(
    fine_feats,
    out_grad,
    pre_act,
    deep_grad,
    down_weight,
    up_weight,
    block_owner,
    parent_slot,
    child_offset,
):
    scene_count = lax.axis_size("scene")
    crop_count = lax.axis_size("crop")
    width = fine_feats.shape[2]
    out_width = pre_act.shape[5]
    capacity = pre_act.shape[3]
    parents = pre_act.shape[4]
    owners = block_owner[0, :, 0]
    blocks = owners.shape[0]
    fine_rows = fine_feats.shape[1]
    rows = fine_rows // blocks
    group = 256 // parents
    steps = blocks // group
    slots = group * parents
    me = lax.axis_index("scene").astype(jnp.uint32)
    peers = [me ^ jnp.uint32(k) for k in range(scene_count)]
    chip_peers = [(me >> 1) ^ jnp.uint32(k) for k in range(scene_count // 2)]
    whole_me = me.astype(jnp.int32)
    ids = jnp.stack([whole_me, whole_me & 1])
    pre_received = exchange(pre_act[0, 0], peers)

    earlier = jnp.arange(blocks)[None, :] < jnp.arange(blocks)[:, None]
    same_owner = owners[:, None] == owners[None, :]
    slot_rank = jnp.sum(same_owner & earlier, axis=1).astype(jnp.int32)
    distance = owners ^ whole_me
    target = distance * capacity + slot_rank
    hit = target[None, :] == jnp.arange(scene_count * capacity, dtype=jnp.int32)[:, None]
    table = jnp.max(jnp.where(hit, jnp.arange(blocks, dtype=jnp.int32)[None, :], -1), axis=1)
    counts = jnp.sum(
        distance[None, :] == jnp.arange(scene_count, dtype=jnp.int32)[:, None], axis=1
    ).astype(jnp.int32)
    table = jnp.concatenate([table, counts])

    places = (child_offset[0] * parents + parent_slot[0]).reshape(steps, group, rows)
    columns = places.transpose(0, 2, 1)
    column_spec = pl.BlockSpec((1, rows, group), lambda g, *_: (g, 0, 0))
    place_spec = pl.BlockSpec((1, group, rows), lambda g, *_: (g, 0, 0))
    fine_spec = pl.BlockSpec((group * rows, width), lambda g, *_: (g, 0))
    coarse_spec = pl.BlockSpec((slots, out_width), lambda g, *_: (g, 0))
    total_rows = blocks * parents
    coarse_f32 = pltpu.VMEM((total_rows, out_width), F32)

    places, columns, ids, table, peers, chip_peers = lax.optimization_barrier(
        (places, columns, ids, table, peers, chip_peers)
    )
    hbm = pl.BlockSpec(memory_space=pltpu.HBM)
    vmem = pl.BlockSpec(memory_space=pltpu.VMEM)
    smem = pl.BlockSpec(memory_space=pltpu.SMEM)
    feat_slots, cot_slots, conv = pl.pallas_call(
        expand_kernel,
        grid=(steps,),
        in_specs=[place_spec, fine_spec, fine_spec, whole_spec(up_weight.shape)],
        out_specs=[vmem] * 3,
        out_shape=[
            pltpu.VMEM((8 * width, total_rows), BF16),
            pltpu.VMEM((total_rows, 8 * width), BF16),
            coarse_f32,
        ],
        scratch_shapes=[
            pltpu.VMEM((out_width, 8 * width), BF16),
            pltpu.VMEM((slots, 8 * width), BF16),
        ],
        compiler_params=grant(12),
    )(places, fine_feats[0], out_grad[0], up_weight)
    deep_whole, conv = lax.optimization_barrier((deep_grad[0, 0], conv))
    deep_received = exchange(deep_whole, peers)

    chips = scene_count // 2

    def dealt(rows, columns):
        shape = (chips, rows, columns)
        return [pltpu.VMEM(shape, F32), pltpu.VMEM(shape, BF16)]

    up_rows, down_rows = 8 * out_width // scene_count, 8 * width // scene_count
    slope, up_mine, up_other = pl.pallas_call(
        lambda *refs: act_kernel(scene_count, *refs),
        in_specs=[smem, smem] + [vmem] * (scene_count + 1),
        out_specs=[vmem] * 3,
        out_shape=[coarse_f32] + dealt(up_rows, width),
        scratch_shapes=[
            pltpu.VMEM((total_rows, out_width), BF16),
            pltpu.VMEM((out_width, 8 * width), F32),
        ],
        compiler_params=grant(12),
    )(table, ids, *pre_received, cot_slots)
    up_part = sum_plane(chip_peers, up_mine, up_other)
    slope, up_part = lax.optimization_barrier((slope, up_part))
    up_done = sum_crops(up_part)

    pre_grad, down_mine, down_other = pl.pallas_call(
        lambda *refs: pre_kernel(scene_count, *refs),
        in_specs=[smem, smem] + [vmem] * (scene_count + 3),
        out_specs=[vmem] * 3,
        out_shape=[pltpu.VMEM((total_rows, out_width), BF16)]
        + dealt(down_rows + BIAS_ROWS, out_width),
        scratch_shapes=[pltpu.VMEM((8 * width, out_width), F32), pltpu.VMEM((8, out_width), F32)],
        compiler_params=grant(12),
    )(table, ids, *deep_received, feat_slots, conv, slope)
    down_part = sum_plane(chip_peers, down_mine, down_other)
    down_done = sum_crops(down_part)
    up_pieces = spread(up_done)
    down_pieces = spread(down_done)

    fine = None
    flat_down = down_weight.reshape(8 * width, out_width)
    for part in range(FINE_PARTS):
        first, count = part * steps // FINE_PARTS, steps // FINE_PARTS
        at = lambda spec: pl.BlockSpec(
            spec.block_shape, lambda g, first=first: (g + first,) + (0,) * (len(spec.block_shape) - 1)
        )
        fine = pl.pallas_call(
            fine_kernel,
            grid=(count,),
            in_specs=[at(column_spec), at(coarse_spec), whole_spec(flat_down.shape)]
            + ([] if part == 0 else [hbm]),
            out_specs=at(fine_spec),
            out_shape=jax.ShapeDtypeStruct((fine_rows, width), BF16),
            input_output_aliases={} if part == 0 else {3: 0},
            compiler_params=grant(12),
        )(columns, pre_grad, flat_down, *([] if part == 0 else [fine]))

    scale = float(crop_count * scene_count * fine_rows) ** (-0.5)
    (up_grad,) = finish(scale, ids, up_pieces, (scene_count, up_rows, width), 0)
    down_grad, bias_grad = finish(scale, ids, down_pieces, (scene_count, down_rows, out_width), 1)
    return (
        fine[None],
        down_grad.reshape(8, width, out_width),
        up_grad.reshape(8, out_width, width),
        bias_grad.reshape(out_width),
    )


def solution(mesh):
    return jax.shard_map(
        on_device,
        mesh=mesh,
        in_specs=(
            P("crop", "scene", None),
            P("crop", "scene", None),
            P("crop", "scene", None, None, None, None),
            P("crop", "scene", None, None, None, None),
            P(),
            P(),
            P("crop", "scene", None),
            P("crop", "scene"),
            P("crop", "scene"),
        ),
        out_specs=(P("crop", "scene", None), P(), P(), P()),
        check_vma=False,
    )
```

```python
import jax
import jax.numpy as jnp
from jax import lax
from jax.experimental import pallas as pl
from jax.experimental.pallas import tpu as pltpu
from jax.sharding import PartitionSpec as P


F32 = jnp.float32
BF16 = jnp.bfloat16
NT = (((1,), (1,)), ((), ()))
TN = (((0,), (0,)), ((), ()))
BIAS_ROWS = 16
FINE_PARTS = 4


def swap(value, axis, step):
    size = lax.axis_size(axis)
    return lax.ppermute(value, axis, [(i, i ^ step) for i in range(size)])


def expand_kernel(places, feats, cotan, up_weight, feat_slots, cot_slots, conv, wide, slot_rows):
    step = pl.program_id(0)
    group = places.shape[1]
    rows, width = feats.shape[0] // group, feats.shape[1]
    parents = slot_rows.shape[0] // group
    slots = slot_rows.shape[0]

    @pl.when(step == 0)
    def _():
        for k in range(8):
            wide[:, k * width : (k + 1) * width] = up_weight[k]

    at = pl.ds(pl.multiple_of(step * slots, slots), slots)
    for i in range(group):
        place = places[0, i : i + 1, :]
        ids = lax.broadcasted_iota(jnp.int32, (parents * 8, rows), 0)
        chooser = jnp.where(ids == place, 1.0, 0.0).astype(BF16)
        both = jnp.concatenate(
            [feats[i * rows : (i + 1) * rows, :], cotan[i * rows : (i + 1) * rows, :]], axis=1
        )
        spread = jnp.dot(chooser, both, preferred_element_type=F32).astype(BF16)
        for k in range(8):
            to = (slice(i * parents, (i + 1) * parents), slice(k * width, (k + 1) * width))
            slot_rows[to] = spread[k * parents : (k + 1) * parents, :width]
            cot_slots[
                pl.ds(pl.multiple_of(step * slots + i * parents, parents), parents),
                k * width : (k + 1) * width,
            ] = spread[k * parents : (k + 1) * parents, width:]
    feat_slots[:, at] = jnp.transpose(slot_rows[...])
    conv[at, :] = lax.dot_general(cot_slots[at, :], wide[...], NT, preferred_element_type=F32)


def each_block(table, received, body):
    capacity = received[0].shape[0]
    for k, ref in enumerate(received):
        count = table[len(received) * capacity + k]

        def one(j, _, k=k, ref=ref):
            body(ref, j, table[k * capacity + j])

        lax.fori_loop(0, count, one, None)


def deal(tiles, ids, mine, other):
    for m, tile in enumerate(tiles):

        @pl.when(ids[1] == m % 2)
        def _():
            mine[m // 2] = tile

        @pl.when(ids[1] != m % 2)
        def _():
            other[m // 2] = tile.astype(BF16)


def act_kernel(count, table, ids, *refs):
    received, (cot_slots, slope, mine, other, act, total) = refs[:count], refs[count:]
    parents = received[0].shape[1]

    def silu(ref, j, block):
        pre = ref[j].astype(F32)
        sig = 0.5 * jnp.tanh(0.5 * pre) + 0.5
        at = pl.ds(pl.multiple_of(block * parents, parents), parents)
        slope[at, :] = sig * (1.0 + pre * (1.0 - sig))
        act[at, :] = (pre * sig).astype(BF16)

    each_block(table, received, silu)
    total[...] = lax.dot_general(act[...], cot_slots[...], TN, preferred_element_type=F32)
    pieces, rows, width = 2 * mine.shape[0], mine.shape[1], mine.shape[2]
    per = pieces // 8
    tiles = [
        total[(m % per) * rows : (m % per + 1) * rows, m // per * width : (m // per + 1) * width]
        for m in range(pieces)
    ]
    deal(tiles, ids, mine, other)


def pre_kernel(count, table, ids, *refs):
    received, rest = refs[:count], refs[count:]
    feat_slots, conv, slope, pre_grad, mine, other, total, bias = rest
    bias[...] = jnp.zeros_like(bias)
    parents = received[0].shape[1]

    def one(ref, j, block):
        at = pl.ds(pl.multiple_of(block * parents, parents), parents)
        grad = ((ref[j].astype(F32) + conv[at, :]) * slope[at, :]).astype(BF16)
        pre_grad[at, :] = grad
        wide = grad.astype(F32)
        bias[...] += jnp.sum(wide.reshape(-1, 8, wide.shape[1]), axis=0)

    each_block(table, received, one)
    total[...] = jnp.dot(feat_slots[...], pre_grad[...], preferred_element_type=F32)
    pieces, width = 2 * mine.shape[0], mine.shape[2]
    rows = total.shape[0] // pieces
    line = jnp.sum(bias[...], axis=0, keepdims=True)
    row = lax.broadcasted_iota(jnp.int32, (BIAS_ROWS, line.shape[1]), 0)
    high = line.astype(BF16).astype(F32)
    extra = jnp.where(row == 0, high, jnp.where(row == 1, line - high, 0.0))
    tiles = [
        jnp.concatenate(
            [
                part
                for at in range(0, line.shape[1], width)
                for part in (
                    total[m * rows : (m + 1) * rows, at : at + width],
                    extra[:, at : at + width],
                )
            ],
            axis=0,
        )
        for m in range(pieces)
    ]
    deal(tiles, ids, mine, other)


def fine_kernel(places, pre_grad, down_weight, *refs):
    fine = refs[-1]
    group = places.shape[2]
    rows, width = fine.shape[0] // group, fine.shape[1]
    parents = pre_grad.shape[0] // group
    slot_grads = lax.dot_general(
        pre_grad[...], down_weight[...], NT, preferred_element_type=F32
    ).astype(BF16)
    for i in range(group):
        slots = lax.broadcasted_iota(jnp.int32, (rows, parents * 8), 1)
        chooser = jnp.where(slots == places[0, :, i : i + 1], 1.0, 0.0).astype(BF16)
        tall = jnp.concatenate(
            [
                slot_grads[i * parents : (i + 1) * parents, k * width : (k + 1) * width]
                for k in range(8)
            ],
            axis=0,
        )
        fine[i * rows : (i + 1) * rows, :] = jnp.dot(
            chooser, tall, preferred_element_type=F32
        ).astype(BF16)


def tree(values):
    while len(values) > 1:
        values = [values[i] + values[i + 1] for i in range(0, len(values), 2)]
    return values[0]


def finish_kernel(scale, ids, *refs):
    *pieces, down_grad, up_grad, bias_grad = refs
    rows, out_width = down_grad.shape[1:]
    up_rows, width = up_grad.shape[1:]
    for i, piece in enumerate(pieces):
        m = ids[0] ^ i
        for at in range(0, out_width, width):
            first = at // width * (rows + BIAS_ROWS)
            down_grad[m, :, at : at + width] = piece[first : first + rows, :].astype(F32) * scale

            @pl.when(m == 0)
            def _():
                pair = piece[first + rows : first + rows + 8, :].astype(F32)
                bias_grad[:, at : at + width] = (pair[0:1] + pair[1:2]) * scale

        first = out_width // width * (rows + BIAS_ROWS)
        up_grad[m] = piece[first : first + up_rows, :].astype(F32) * scale


def grant(mebibytes):
    return pltpu.CompilerParams(vmem_limit_bytes=mebibytes << 20)


def whole_spec(shape):
    return pl.BlockSpec(shape, lambda *_: (0,) * len(shape))


def finish(scale, ids, pieces, down_shape, up_shape):
    outputs = [
        jax.ShapeDtypeStruct(shape, F32) for shape in (down_shape, up_shape, (1, down_shape[2]))
    ]
    return pl.pallas_call(
        lambda *refs: finish_kernel(scale, *refs),
        grid_spec=pltpu.PrefetchScalarGridSpec(
            num_scalar_prefetch=1,
            grid=(1,),
            in_specs=[whole_spec(x.shape) for x in pieces],
            out_specs=[whole_spec(x.shape) for x in outputs],
        ),
        out_shape=outputs,
        compiler_params=grant(12),
    )(ids, *pieces)


def row_of(array, index):
    start = (index,) + (jnp.uint32(0),) * (array.ndim - 1)
    return lax.dynamic_slice(array, start, (1,) + array.shape[1:])[0]


def sum_plane(peers, mine, other):
    chips = mine.shape[0]
    arrived = swap(other, "scene", 1)

    def both(peer):
        return row_of(mine, peer) + row_of(arrived, peer).astype(F32)

    sends = {d: both(peers[d]).astype(BF16) for d in range(1, chips)}
    parts = {d: swap(sends[d], "scene", 2 * d) for d in far_first(chips)}
    return tree([both(peers[0])] + [parts[d].astype(F32) for d in range(1, chips)]).astype(BF16)


def far_first(count):
    return sorted(range(1, count), key=lambda d: -bin(d).count("1"))


def sum_crops(part):
    crops = lax.axis_size("crop")
    parts = {d: swap(part, "crop", d) for d in far_first(crops)}
    return tree([part.astype(F32)] + [parts[d].astype(F32) for d in range(1, crops)]).astype(BF16)


def spread(done):
    chips = lax.axis_size("scene") // 2
    even = {d: swap(done, "scene", 2 * d) for d in far_first(chips)}
    even[0] = done
    odd = {d: swap(even[d], "scene", 1) for d in range(chips)}
    return [x for d in range(chips) for x in (even[d], odd[d])]


def cut(array, ids, distances):
    def kernel(ids, array, *refs):
        *parts, sems = refs
        copies = [
            pltpu.make_async_copy(array.at[ids[0] ^ k], part, sems.at[i])
            for i, (k, part) in enumerate(zip(distances, parts))
        ]
        for copy in copies:
            copy.start()
        for copy in copies:
            copy.wait()

    return pl.pallas_call(
        kernel,
        in_specs=[
            pl.BlockSpec(memory_space=pltpu.SMEM),
            pl.BlockSpec(memory_space=pltpu.HBM),
        ],
        out_specs=[pl.BlockSpec(memory_space=pltpu.VMEM)] * len(distances),
        out_shape=[pltpu.VMEM(array.shape[1:], array.dtype)] * len(distances),
        scratch_shapes=[pltpu.SemaphoreType.DMA((len(distances),))],
        compiler_params=grant(12),
    )(ids, pltpu.with_memory_space_constraint(array, pltpu.HBM))


def exchange(array, ids, groups):
    out = {}
    for group in groups:
        for k, part in zip(group, cut(array, ids, group)):
            out[k] = part if k == 0 else swap(part, "scene", k)
    return [out[k] for k in range(array.shape[0])]


def exchange_order(count):
    return [2, 4, 6, 3, 5, 7, 1] if count == 8 else list(range(1, count))


def on_device(
    fine_feats,
    out_grad,
    pre_act,
    deep_grad,
    down_weight,
    up_weight,
    block_owner,
    parent_slot,
    child_offset,
):
    scene_count = lax.axis_size("scene")
    crop_count = lax.axis_size("crop")
    width = fine_feats.shape[2]
    out_width = pre_act.shape[5]
    capacity = pre_act.shape[3]
    parents = pre_act.shape[4]
    owners = block_owner[0, :, 0]
    blocks = owners.shape[0]
    fine_rows = fine_feats.shape[1]
    rows = fine_rows // blocks
    group = 256 // parents
    steps = blocks // group
    slots = group * parents
    me = lax.axis_index("scene").astype(jnp.uint32)
    chip_peers = [(me >> 1) ^ jnp.uint32(k) for k in range(scene_count // 2)]
    whole_me = me.astype(jnp.int32)
    ids = jnp.stack([whole_me, whole_me & 1])
    order = exchange_order(scene_count)
    pre_received = exchange(pre_act[0, 0], ids, [order[:2], order[2:] + [0]])

    earlier = jnp.arange(blocks)[None, :] < jnp.arange(blocks)[:, None]
    same_owner = owners[:, None] == owners[None, :]
    slot_rank = jnp.sum(same_owner & earlier, axis=1).astype(jnp.int32)
    distance = owners ^ whole_me
    target = distance * capacity + slot_rank
    hit = target[None, :] == jnp.arange(scene_count * capacity, dtype=jnp.int32)[:, None]
    table = jnp.max(jnp.where(hit, jnp.arange(blocks, dtype=jnp.int32)[None, :], -1), axis=1)
    counts = jnp.sum(
        distance[None, :] == jnp.arange(scene_count, dtype=jnp.int32)[:, None], axis=1
    ).astype(jnp.int32)
    table = jnp.concatenate([table, counts])

    places = (child_offset[0] * parents + parent_slot[0]).reshape(steps, group, rows)
    columns = places.transpose(0, 2, 1)
    column_spec = pl.BlockSpec((1, rows, group), lambda g, *_: (g, 0, 0))
    place_spec = pl.BlockSpec((1, group, rows), lambda g, *_: (g, 0, 0))
    fine_spec = pl.BlockSpec((group * rows, width), lambda g, *_: (g, 0))
    coarse_spec = pl.BlockSpec((slots, out_width), lambda g, *_: (g, 0))
    total_rows = blocks * parents
    coarse_f32 = pltpu.VMEM((total_rows, out_width), F32)

    places, columns, ids, table, chip_peers = lax.optimization_barrier(
        (places, columns, ids, table, chip_peers)
    )
    hbm = pl.BlockSpec(memory_space=pltpu.HBM)
    vmem = pl.BlockSpec(memory_space=pltpu.VMEM)
    smem = pl.BlockSpec(memory_space=pltpu.SMEM)
    feat_slots, cot_slots, conv = pl.pallas_call(
        expand_kernel,
        grid=(steps,),
        in_specs=[place_spec, fine_spec, fine_spec, whole_spec(up_weight.shape)],
        out_specs=[vmem] * 3,
        out_shape=[
            pltpu.VMEM((8 * width, total_rows), BF16),
            pltpu.VMEM((total_rows, 8 * width), BF16),
            coarse_f32,
        ],
        scratch_shapes=[
            pltpu.VMEM((out_width, 8 * width), BF16),
            pltpu.VMEM((slots, 8 * width), BF16),
        ],
        compiler_params=grant(12),
    )(
        places,
        pltpu.with_memory_space_constraint(fine_feats[0], pltpu.HBM),
        pltpu.with_memory_space_constraint(out_grad[0], pltpu.HBM),
        up_weight,
    )
    deep_whole, conv = lax.optimization_barrier((deep_grad[0, 0], conv))
    deep_received = exchange(deep_whole, ids, [order + [0]])

    chips = scene_count // 2

    def dealt(rows, columns):
        shape = (chips, rows, columns)
        return [pltpu.VMEM(shape, F32), pltpu.VMEM(shape, BF16)]

    up_rows, down_rows = 8 * out_width // scene_count, 8 * width // scene_count
    slope, up_mine, up_other = pl.pallas_call(
        lambda *refs: act_kernel(scene_count, *refs),
        in_specs=[smem, smem] + [vmem] * (scene_count + 1),
        out_specs=[vmem] * 3,
        out_shape=[coarse_f32] + dealt(up_rows, width),
        scratch_shapes=[
            pltpu.VMEM((total_rows, out_width), BF16),
            pltpu.VMEM((out_width, 8 * width), F32),
        ],
        compiler_params=grant(12),
    )(table, ids, *pre_received, cot_slots)
    up_part = sum_plane(chip_peers, up_mine, up_other)
    slope, up_part = lax.optimization_barrier((slope, up_part))
    up_done = sum_crops(up_part)

    pre_grad, down_mine, down_other = pl.pallas_call(
        lambda *refs: pre_kernel(scene_count, *refs),
        in_specs=[smem, smem] + [vmem] * (scene_count + 3),
        out_specs=[vmem] * 3,
        out_shape=[pltpu.VMEM((total_rows, out_width), BF16)]
        + dealt(out_width // width * (down_rows + BIAS_ROWS), width),
        scratch_shapes=[pltpu.VMEM((8 * width, out_width), F32), pltpu.VMEM((8, out_width), F32)],
        compiler_params=grant(12),
    )(table, ids, *deep_received, feat_slots, conv, slope)
    down_part = sum_plane(chip_peers, down_mine, down_other)
    down_done = sum_crops(down_part)
    pieces = spread(jnp.concatenate([down_done, up_done]))

    fine = None
    flat_down = down_weight.reshape(8 * width, out_width)
    for part in range(FINE_PARTS):
        first, count = part * steps // FINE_PARTS, steps // FINE_PARTS
        at = lambda spec: pl.BlockSpec(
            spec.block_shape, lambda g, first=first: (g + first,) + (0,) * (len(spec.block_shape) - 1)
        )
        fine = pl.pallas_call(
            fine_kernel,
            grid=(count,),
            in_specs=[at(column_spec), at(coarse_spec), whole_spec(flat_down.shape)]
            + ([] if part == 0 else [hbm]),
            out_specs=at(fine_spec),
            out_shape=jax.ShapeDtypeStruct((fine_rows, width), BF16),
            input_output_aliases={} if part == 0 else {3: 0},
            compiler_params=grant(12),
        )(columns, pre_grad, flat_down, *([] if part == 0 else [fine]))

    scale = float(crop_count * scene_count * fine_rows) ** (-0.5)
    down_grad, up_grad, bias_grad = finish(
        scale,
        ids,
        pieces,
        (scene_count, down_rows, out_width),
        (scene_count, up_rows, width),
    )
    return (
        fine[None],
        down_grad.reshape(8, width, out_width),
        up_grad.reshape(8, out_width, width),
        bias_grad.reshape(out_width),
    )


def solution(mesh):
    return jax.shard_map(
        on_device,
        mesh=mesh,
        in_specs=(
            P("crop", "scene", None),
            P("crop", "scene", None),
            P("crop", "scene", None, None, None, None),
            P("crop", "scene", None, None, None, None),
            P(),
            P(),
            P("crop", "scene", None),
            P("crop", "scene"),
            P("crop", "scene"),
        ),
        out_specs=(P("crop", "scene", None), P(), P(), P()),
        check_vma=False,
    )
```

```python
import jax
import jax.numpy as jnp
from jax import lax
from jax.experimental import pallas as pl
from jax.experimental.pallas import tpu as pltpu
from jax.sharding import PartitionSpec as P


F32 = jnp.float32
BF16 = jnp.bfloat16
NT = (((1,), (1,)), ((), ()))
TN = (((0,), (0,)), ((), ()))
BIAS_ROWS = 16
FINE_SHARES = (8, 8, 8, 8)


def swap(value, axis, step):
    size = lax.axis_size(axis)
    return lax.ppermute(value, axis, [(i, i ^ step) for i in range(size)])


def expand_kernel(places, feats, cotan, up_weight, feat_slots, cot_slots, conv, wide, slot_rows):
    step = pl.program_id(0)
    group = places.shape[1]
    rows, width = feats.shape[0] // group, feats.shape[1]
    parents = slot_rows.shape[0] // group
    slots = slot_rows.shape[0]

    @pl.when(step == 0)
    def _():
        for k in range(8):
            wide[:, k * width : (k + 1) * width] = up_weight[k]

    at = pl.ds(pl.multiple_of(step * slots, slots), slots)
    for i in range(group):
        place = places[0, i : i + 1, :]
        ids = lax.broadcasted_iota(jnp.int32, (parents * 8, rows), 0)
        chooser = jnp.where(ids == place, 1.0, 0.0).astype(BF16)
        both = jnp.concatenate(
            [feats[i * rows : (i + 1) * rows, :], cotan[i * rows : (i + 1) * rows, :]], axis=1
        )
        spread = jnp.dot(chooser, both, preferred_element_type=F32).astype(BF16)
        for k in range(8):
            to = (slice(i * parents, (i + 1) * parents), slice(k * width, (k + 1) * width))
            slot_rows[to] = spread[k * parents : (k + 1) * parents, :width]
            cot_slots[
                pl.ds(pl.multiple_of(step * slots + i * parents, parents), parents),
                k * width : (k + 1) * width,
            ] = spread[k * parents : (k + 1) * parents, width:]
    feat_slots[:, at] = jnp.transpose(slot_rows[...])
    conv[at, :] = lax.dot_general(cot_slots[at, :], wide[...], NT, preferred_element_type=F32)


def each_block(table, received, body):
    capacity = received[0].shape[0]
    for k, ref in enumerate(received):
        count = table[len(received) * capacity + k]

        def one(j, _, k=k, ref=ref):
            body(ref, j, table[k * capacity + j])

        lax.fori_loop(0, count, one, None)


def deal(tiles, ids, mine, other):
    for m, tile in enumerate(tiles):

        @pl.when(ids[1] == m % 2)
        def _():
            mine[m // 2] = tile

        @pl.when(ids[1] != m % 2)
        def _():
            other[m // 2] = tile.astype(BF16)


def act_kernel(count, table, ids, *refs):
    received, (cot_slots, slope, mine, other, act, total) = refs[:count], refs[count:]
    parents = received[0].shape[1]

    def silu(ref, j, block):
        pre = ref[j].astype(F32)
        sig = 0.5 * jnp.tanh(0.5 * pre) + 0.5
        at = pl.ds(pl.multiple_of(block * parents, parents), parents)
        slope[at, :] = sig * (1.0 + pre * (1.0 - sig))
        act[at, :] = (pre * sig).astype(BF16)

    each_block(table, received, silu)
    total[...] = lax.dot_general(act[...], cot_slots[...], TN, preferred_element_type=F32)
    pieces, rows, width = 2 * mine.shape[0], mine.shape[1], mine.shape[2]
    per = pieces // 8
    tiles = [
        total[(m % per) * rows : (m % per + 1) * rows, m // per * width : (m // per + 1) * width]
        for m in range(pieces)
    ]
    deal(tiles, ids, mine, other)


def pre_kernel(count, table, ids, *refs):
    received, rest = refs[:count], refs[count:]
    feat_slots, conv, slope, pre_grad, other, extra, bias = rest
    bias[...] = jnp.zeros_like(bias)
    parents = received[0].shape[1]

    def one(ref, j, block):
        at = pl.ds(pl.multiple_of(block * parents, parents), parents)
        grad = ((ref[j].astype(F32) + conv[at, :]) * slope[at, :]).astype(BF16)
        pre_grad[at, :] = grad
        wide = grad.astype(F32)
        bias[...] += jnp.sum(wide.reshape(-1, 8, wide.shape[1]), axis=0)

    each_block(table, received, one)
    line = jnp.sum(bias[...], axis=0, keepdims=True)
    high = line.astype(BF16).astype(F32)
    width = extra.shape[1]
    extra[...] = jnp.zeros_like(extra)
    for i, part in enumerate((high, line - high)):
        for j in range(line.shape[1] // width):
            at = i * (line.shape[1] // width) + j
            extra[at : at + 1, :] = part[:, j * width : (j + 1) * width]
    down_pieces(1 - ids[1], feat_slots, pre_grad, extra, other)


def own_kernel(ids, feat_slots, pre_grad, extra, mine):
    down_pieces(ids[1], feat_slots, pre_grad, extra, mine)


def down_pieces(core, feat_slots, pre_grad, extra, out):
    chips, _, width = out.shape
    rows = feat_slots.shape[0] // (2 * chips)
    lines = [
        feat_slots[pl.ds(pl.multiple_of((2 * i + core) * rows, rows), rows), :]
        for i in range(chips)
    ]
    total = jnp.dot(jnp.concatenate(lines, axis=0), pre_grad[...], preferred_element_type=F32)
    for i in range(chips):
        for j in range(total.shape[1] // width):
            tile = total[i * rows : (i + 1) * rows, j * width : (j + 1) * width]
            out[i, j * rows : (j + 1) * rows, :] = tile.astype(out.dtype)
        out[i, out.shape[1] - BIAS_ROWS :, :] = extra[...].astype(out.dtype)


def prepare_kernel(
    parents, parent_slot, child_offset, down_weight, places, columns, down_wide, flat
):
    steps, group, rows = places.shape
    flat[...] = jnp.zeros_like(flat)
    for block in range(steps * group):
        at = slice(block * rows, (block + 1) * rows)
        place = child_offset[0:1, at] * parents + parent_slot[0:1, at]
        places[block // group, block % group : block % group + 1, :] = place
        flat[block : block + 1, :rows] = place
    columns[...] = jnp.transpose(flat[...])
    width = down_weight.shape[1]
    for k in range(8):
        down_wide[:, k * width : (k + 1) * width] = jnp.transpose(down_weight[k])


def fine_kernel(first, group, parents, columns, pre_grad, down_wide, *refs):
    fine = refs[-1]
    rows, width = fine.shape[0] * parents // pre_grad.shape[0], fine.shape[1]
    grads = pre_grad[first * parents : (first + group) * parents, :]
    slot_grads = jnp.dot(grads, down_wide[...], preferred_element_type=F32).astype(BF16)
    for i in range(group):
        slots = lax.broadcasted_iota(jnp.int32, (rows, parents * 8), 1)
        place = columns[:rows, first + i : first + i + 1]
        chooser = jnp.where(slots == place, 1.0, 0.0).astype(BF16)
        tall = jnp.concatenate(
            [
                slot_grads[i * parents : (i + 1) * parents, k * width : (k + 1) * width]
                for k in range(8)
            ],
            axis=0,
        )
        fine[(first + i) * rows : (first + i + 1) * rows, :] = jnp.dot(
            chooser, tall, preferred_element_type=F32
        ).astype(BF16)


def tree(values):
    while len(values) > 1:
        values = [values[i] + values[i + 1] for i in range(0, len(values), 2)]
    return values[0]


def up_end_kernel(scale, ids, *refs):
    *pieces, up_grad = refs
    for i, piece in enumerate(pieces):
        up_grad[ids[0] ^ i] = piece[...].astype(F32) * scale


def down_end_kernel(scale, ids, *refs):
    *pieces, down_grad, bias_grad = refs
    rows, out_width = down_grad.shape[1:]
    width = pieces[0].shape[1]
    for i, piece in enumerate(pieces):
        m = ids[0] ^ i
        parts = out_width // width
        for j in range(parts):
            tile = piece[j * rows : (j + 1) * rows, :].astype(F32)
            down_grad[m, :, j * width : (j + 1) * width] = tile * scale

        @pl.when(m == 0)
        def _():
            lines = piece[parts * rows :, :].astype(F32)
            for j in range(parts):
                pair = lines[j : j + 1] + lines[parts + j : parts + j + 1]
                bias_grad[:, j * width : (j + 1) * width] = pair * scale


def finish(kernel, ids, pieces, shapes):
    vmem = pl.BlockSpec(memory_space=pltpu.VMEM)
    return pl.pallas_call(
        kernel,
        grid_spec=pltpu.PrefetchScalarGridSpec(
            num_scalar_prefetch=1,
            grid=(1,),
            in_specs=[vmem] * len(pieces),
            out_specs=[whole_spec(shape) for shape in shapes],
        ),
        out_shape=[jax.ShapeDtypeStruct(shape, F32) for shape in shapes],
        compiler_params=grant(12),
    )(ids, *pieces)


def grant(mebibytes):
    return pltpu.CompilerParams(vmem_limit_bytes=mebibytes << 20)


def whole_spec(shape):
    return pl.BlockSpec(shape, lambda *_: (0,) * len(shape))


def row_of(array, index):
    start = (index,) + (jnp.uint32(0),) * (array.ndim - 1)
    return lax.dynamic_slice(array, start, (1,) + array.shape[1:])[0]


def sum_plane(peers, mine, other):
    chips = mine.shape[0]
    arrived = swap(other, "scene", 1)

    def both(peer):
        return row_of(mine, peer) + row_of(arrived, peer).astype(F32)

    sends = {d: both(peers[d]).astype(BF16) for d in range(1, chips)}
    parts = {d: swap(sends[d], "scene", 2 * d) for d in far_first(chips)}
    return tree([both(peers[0])] + [parts[d].astype(F32) for d in range(1, chips)]).astype(BF16)


def far_first(count):
    return sorted(range(1, count), key=lambda d: -bin(d).count("1"))


def crop_order(count):
    return [2, 3, 1] if count == 4 else far_first(count)


def sum_crops(part):
    crops = lax.axis_size("crop")
    parts = {d: swap(part, "crop", d) for d in crop_order(crops)}
    return tree([part.astype(F32)] + [parts[d].astype(F32) for d in range(1, crops)]).astype(BF16)


def spread(done):
    chips = lax.axis_size("scene") // 2
    even = {d: swap(done, "scene", 2 * d) for d in far_first(chips)}
    even[0] = done
    odd = {d: swap(even[d], "scene", 1) for d in range(chips)}
    return [x for d in range(chips) for x in (even[d], odd[d])]


def cut(array, ids, distances):
    def kernel(ids, array, *refs):
        *parts, sems = refs
        copies = [
            pltpu.make_async_copy(array.at[ids[0] ^ k], part, sems.at[i])
            for i, (k, part) in enumerate(zip(distances, parts))
        ]
        for copy in copies:
            copy.start()
        for copy in copies:
            copy.wait()

    return pl.pallas_call(
        kernel,
        in_specs=[
            pl.BlockSpec(memory_space=pltpu.SMEM),
            pl.BlockSpec(memory_space=pltpu.HBM),
        ],
        out_specs=[pl.BlockSpec(memory_space=pltpu.VMEM)] * len(distances),
        out_shape=[pltpu.VMEM(array.shape[1:], array.dtype)] * len(distances),
        scratch_shapes=[pltpu.SemaphoreType.DMA((len(distances),))],
        compiler_params=grant(12),
    )(ids, pltpu.with_memory_space_constraint(array, pltpu.HBM))


def exchange(array, ids, groups):
    out = {}
    for group in groups:
        for k, part in zip(group, cut(array, ids, group)):
            out[k] = part if k == 0 else swap(part, "scene", k)
    return [out[k] for k in range(array.shape[0])]


def exchange_order(count):
    return [2, 4, 6, 3, 5, 7, 1] if count == 8 else list(range(1, count))


def on_device(
    fine_feats,
    out_grad,
    pre_act,
    deep_grad,
    down_weight,
    up_weight,
    block_owner,
    parent_slot,
    child_offset,
):
    scene_count = lax.axis_size("scene")
    crop_count = lax.axis_size("crop")
    width = fine_feats.shape[2]
    out_width = pre_act.shape[5]
    capacity = pre_act.shape[3]
    parents = pre_act.shape[4]
    owners = block_owner[0, :, 0]
    blocks = owners.shape[0]
    fine_rows = fine_feats.shape[1]
    rows = fine_rows // blocks
    group = 256 // parents
    steps = blocks // group
    slots = group * parents
    me = lax.axis_index("scene").astype(jnp.uint32)
    chip_peers = [(me >> 1) ^ jnp.uint32(k) for k in range(scene_count // 2)]
    whole_me = me.astype(jnp.int32)
    ids = jnp.stack([whole_me, whole_me & 1])
    ids, chip_peers = lax.optimization_barrier((ids, chip_peers))
    order = exchange_order(scene_count)
    pre_received = exchange(pre_act[0, 0], ids, [order[:2], order[2:] + [0]])

    earlier = jnp.arange(blocks)[None, :] < jnp.arange(blocks)[:, None]
    same_owner = owners[:, None] == owners[None, :]
    slot_rank = jnp.sum(same_owner & earlier, axis=1).astype(jnp.int32)
    distance = owners ^ whole_me
    target = distance * capacity + slot_rank
    hit = target[None, :] == jnp.arange(scene_count * capacity, dtype=jnp.int32)[:, None]
    table = jnp.max(jnp.where(hit, jnp.arange(blocks, dtype=jnp.int32)[None, :], -1), axis=1)
    counts = jnp.sum(
        distance[None, :] == jnp.arange(scene_count, dtype=jnp.int32)[:, None], axis=1
    ).astype(jnp.int32)
    table = jnp.concatenate([table, counts])

    ids, table, chip_peers = lax.optimization_barrier((ids, table, chip_peers))
    lanes = -(-rows // 128) * 128
    vmem = pl.BlockSpec(memory_space=pltpu.VMEM)
    places, columns, down_wide = pl.pallas_call(
        lambda *refs: prepare_kernel(parents, *refs),
        in_specs=[vmem] * 3,
        out_specs=[vmem] * 3,
        out_shape=[
            jax.ShapeDtypeStruct((steps, group, rows), jnp.int32),
            pltpu.VMEM((lanes, blocks), jnp.int32),
            pltpu.VMEM((out_width, 8 * width), BF16),
        ],
        scratch_shapes=[pltpu.VMEM((blocks, lanes), jnp.int32)],
        compiler_params=grant(12),
    )(parent_slot, child_offset, down_weight)
    place_spec = pl.BlockSpec((1, group, rows), lambda g, *_: (g, 0, 0))
    fine_spec = pl.BlockSpec((group * rows, width), lambda g, *_: (g, 0))
    coarse_spec = pl.BlockSpec((slots, out_width), lambda g, *_: (g, 0))
    total_rows = blocks * parents
    coarse_f32 = pltpu.VMEM((total_rows, out_width), F32)

    hbm = pl.BlockSpec(memory_space=pltpu.HBM)
    smem = pl.BlockSpec(memory_space=pltpu.SMEM)
    feat_slots, cot_slots, conv = pl.pallas_call(
        expand_kernel,
        grid=(steps,),
        in_specs=[place_spec, fine_spec, fine_spec, whole_spec(up_weight.shape)],
        out_specs=[vmem] * 3,
        out_shape=[
            pltpu.VMEM((8 * width, total_rows), BF16),
            pltpu.VMEM((total_rows, 8 * width), BF16),
            coarse_f32,
        ],
        scratch_shapes=[
            pltpu.VMEM((out_width, 8 * width), BF16),
            pltpu.VMEM((slots, 8 * width), BF16),
        ],
        compiler_params=grant(12),
    )(
        places,
        pltpu.with_memory_space_constraint(fine_feats[0], pltpu.HBM),
        pltpu.with_memory_space_constraint(out_grad[0], pltpu.HBM),
        up_weight,
    )
    deep_whole, conv = lax.optimization_barrier((deep_grad[0, 0], conv))
    deep_received = exchange(deep_whole, ids, [order + [0]])

    chips = scene_count // 2

    def dealt(rows, columns):
        shape = (chips, rows, columns)
        return [pltpu.VMEM(shape, F32), pltpu.VMEM(shape, BF16)]

    up_rows, down_rows = 8 * out_width // scene_count, 8 * width // scene_count
    slope, up_mine, up_other = pl.pallas_call(
        lambda *refs: act_kernel(scene_count, *refs),
        in_specs=[smem, smem] + [vmem] * (scene_count + 1),
        out_specs=[vmem] * 3,
        out_shape=[coarse_f32] + dealt(up_rows, width),
        scratch_shapes=[
            pltpu.VMEM((total_rows, out_width), BF16),
            pltpu.VMEM((out_width, 8 * width), F32),
        ],
        compiler_params=grant(12),
    )(table, ids, *pre_received, cot_slots)
    up_part = sum_plane(chip_peers, up_mine, up_other)
    slope, up_part = lax.optimization_barrier((slope, up_part))
    up_done = sum_crops(up_part)

    mine_shape, other_shape = dealt(
        out_width // width * down_rows + BIAS_ROWS, width
    )
    pre_grad, down_other, extra = pl.pallas_call(
        lambda *refs: pre_kernel(scene_count, *refs),
        in_specs=[smem, smem] + [vmem] * (scene_count + 3),
        out_specs=[vmem] * 3,
        out_shape=[
            pltpu.VMEM((total_rows, out_width), BF16),
            other_shape,
            pltpu.VMEM((BIAS_ROWS, width), F32),
        ],
        scratch_shapes=[pltpu.VMEM((8, out_width), F32)],
        compiler_params=grant(12),
    )(table, ids, *deep_received, feat_slots, conv, slope)
    down_mine = pl.pallas_call(
        own_kernel,
        in_specs=[smem] + [vmem] * 3,
        out_specs=vmem,
        out_shape=mine_shape,
        compiler_params=grant(12),
    )(ids, feat_slots, pre_grad, extra)
    down_part = sum_plane(chip_peers, down_mine, down_other)
    down_done = sum_crops(down_part)
    down_pieces = spread(down_done)
    up_pieces = spread(up_done)

    fine = None
    first = 0
    for part, share in enumerate(FINE_SHARES):
        group = blocks * share // sum(FINE_SHARES)
        held = [] if part == 0 else [fine]
        fine = pl.pallas_call(
            lambda *refs, first=first, group=group: fine_kernel(first, group, parents, *refs),
            in_specs=[vmem] * (3 + len(held)),
            out_specs=vmem,
            out_shape=pltpu.VMEM((fine_rows, width), BF16),
            input_output_aliases={3: 0} if held else {},
            compiler_params=grant(12),
        )(columns, pre_grad, down_wide, *held)
        first += group

    scale = float(crop_count * scene_count * fine_rows) ** (-0.5)
    (up_grad,) = finish(
        lambda *refs: up_end_kernel(scale, *refs),
        ids,
        up_pieces,
        [(scene_count, up_rows, width)],
    )
    down_grad, bias_grad = finish(
        lambda *refs: down_end_kernel(scale, *refs),
        ids,
        down_pieces,
        [(scene_count, down_rows, out_width), (1, out_width)],
    )
    return (
        fine[None],
        down_grad.reshape(8, width, out_width),
        up_grad.reshape(8, out_width, width),
        bias_grad.reshape(out_width),
    )


def solution(mesh):
    return jax.shard_map(
        on_device,
        mesh=mesh,
        in_specs=(
            P("crop", "scene", None),
            P("crop", "scene", None),
            P("crop", "scene", None, None, None, None),
            P("crop", "scene", None, None, None, None),
            P(),
            P(),
            P("crop", "scene", None),
            P("crop", "scene"),
            P("crop", "scene"),
        ),
        out_specs=(P("crop", "scene", None), P(), P(), P()),
        check_vma=False,
    )
```

```python
import jax
import jax.numpy as jnp
from jax import lax
from jax.experimental import pallas as pl
from jax.experimental.pallas import tpu as pltpu
from jax.sharding import PartitionSpec as P


F32 = jnp.float32
BF16 = jnp.bfloat16
NT = (((1,), (1,)), ((), ()))
TN = (((0,), (0,)), ((), ()))
BIAS_ROWS = 16
FINE_SHARES = (8, 8, 8, 8)
HELD_BACK = [7, 5]


def swap(value, axis, step):
    size = lax.axis_size(axis)
    return lax.ppermute(value, axis, [(i, i ^ step) for i in range(size)])


def expand_kernel(places, feats, cotan, up_weight, feat_slots, cot_slots, conv, wide, slot_rows):
    step = pl.program_id(0)
    group = places.shape[1]
    rows, width = feats.shape[0] // group, feats.shape[1]
    parents = slot_rows.shape[0] // group
    slots = slot_rows.shape[0]

    @pl.when(step == 0)
    def _():
        for k in range(8):
            wide[:, k * width : (k + 1) * width] = up_weight[k]

    at = pl.ds(pl.multiple_of(step * slots, slots), slots)
    for i in range(group):
        place = places[0, i : i + 1, :]
        ids = lax.broadcasted_iota(jnp.int32, (parents * 8, rows), 0)
        chooser = jnp.where(ids == place, 1.0, 0.0).astype(BF16)
        both = jnp.concatenate(
            [feats[i * rows : (i + 1) * rows, :], cotan[i * rows : (i + 1) * rows, :]], axis=1
        )
        spread = jnp.dot(chooser, both, preferred_element_type=F32).astype(BF16)
        for k in range(8):
            to = (slice(i * parents, (i + 1) * parents), slice(k * width, (k + 1) * width))
            slot_rows[to] = spread[k * parents : (k + 1) * parents, :width]
            cot_slots[
                pl.ds(pl.multiple_of(step * slots + i * parents, parents), parents),
                k * width : (k + 1) * width,
            ] = spread[k * parents : (k + 1) * parents, width:]
    feat_slots[:, at] = jnp.transpose(slot_rows[...])
    conv[at, :] = lax.dot_general(cot_slots[at, :], wide[...], NT, preferred_element_type=F32)


def each_block(table, count, received, body):
    for k, ref in received.items():
        capacity = ref.shape[0]

        def one(j, _, k=k, ref=ref, capacity=capacity):
            body(ref, j, table[k * capacity + j])

        lax.fori_loop(0, table[count * capacity + k], one, None)


def deal(tiles, ids, mine, other):
    for m, tile in enumerate(tiles):

        @pl.when(ids[1] == m % 2)
        def _():
            mine[m // 2] = tile

        @pl.when(ids[1] != m % 2)
        def _():
            other[m // 2] = tile.astype(BF16)


def act_kernel(count, table, ids, *refs):
    received, (cot_slots, slope, mine, other, act, total) = refs[:count], refs[count:]
    parents = received[0].shape[1]

    def silu(ref, j, block):
        pre = ref[j].astype(F32)
        sig = 0.5 * jnp.tanh(0.5 * pre) + 0.5
        at = pl.ds(pl.multiple_of(block * parents, parents), parents)
        slope[at, :] = sig * (1.0 + pre * (1.0 - sig))
        act[at, :] = (pre * sig).astype(BF16)

    each_block(table, count, dict(enumerate(received)), silu)
    total[...] = lax.dot_general(act[...], cot_slots[...], TN, preferred_element_type=F32)
    pieces, rows, width = 2 * mine.shape[0], mine.shape[1], mine.shape[2]
    per = pieces // 8
    tiles = [
        total[(m % per) * rows : (m % per + 1) * rows, m // per * width : (m // per + 1) * width]
        for m in range(pieces)
    ]
    deal(tiles, ids, mine, other)


def grad_blocks(table, count, received, conv, slope, pre_grad, bias):
    def one(ref, j, block):
        parents = ref.shape[1]
        at = pl.ds(pl.multiple_of(block * parents, parents), parents)
        grad = ((ref[j].astype(F32) + conv[at, :]) * slope[at, :]).astype(BF16)
        pre_grad[at, :] = grad
        wide = grad.astype(F32)
        bias[...] += jnp.sum(wide.reshape(-1, 8, wide.shape[1]), axis=0)

    each_block(table, count, received, one)


def early_kernel(count, distances, table, *refs):
    *received, conv, slope, pre_grad, bias = refs
    bias[...] = jnp.zeros_like(bias)
    grad_blocks(table, count, dict(zip(distances, received)), conv, slope, pre_grad, bias)


def pre_kernel(count, distances, table, ids, *refs):
    received, rest = refs[: len(distances)], refs[len(distances) :]
    feat_slots, conv, slope, _, half_bias, pre_grad, other, extra, bias = rest
    bias[...] = half_bias[...]
    grad_blocks(table, count, dict(zip(distances, received)), conv, slope, pre_grad, bias)
    line = jnp.sum(bias[...], axis=0, keepdims=True)
    high = line.astype(BF16).astype(F32)
    width = extra.shape[1]
    extra[...] = jnp.zeros_like(extra)
    for i, part in enumerate((high, line - high)):
        for j in range(line.shape[1] // width):
            at = i * (line.shape[1] // width) + j
            extra[at : at + 1, :] = part[:, j * width : (j + 1) * width]
    down_pieces(1 - ids[1], feat_slots, pre_grad, extra, other)


def own_kernel(ids, feat_slots, pre_grad, extra, mine):
    down_pieces(ids[1], feat_slots, pre_grad, extra, mine)


def down_pieces(core, feat_slots, pre_grad, extra, out):
    chips, _, width = out.shape
    rows = feat_slots.shape[0] // (2 * chips)
    lines = [
        feat_slots[pl.ds(pl.multiple_of((2 * i + core) * rows, rows), rows), :]
        for i in range(chips)
    ]
    total = jnp.dot(jnp.concatenate(lines, axis=0), pre_grad[...], preferred_element_type=F32)
    for i in range(chips):
        for j in range(total.shape[1] // width):
            tile = total[i * rows : (i + 1) * rows, j * width : (j + 1) * width]
            out[i, j * rows : (j + 1) * rows, :] = tile.astype(out.dtype)
        out[i, out.shape[1] - BIAS_ROWS :, :] = extra[...].astype(out.dtype)


def prepare_kernel(
    parents, parent_slot, child_offset, down_weight, places, columns, down_wide, flat
):
    steps, group, rows = places.shape
    flat[...] = jnp.zeros_like(flat)
    for block in range(steps * group):
        at = slice(block * rows, (block + 1) * rows)
        place = child_offset[0:1, at] * parents + parent_slot[0:1, at]
        places[block // group, block % group : block % group + 1, :] = place
        flat[block : block + 1, :rows] = place
    columns[...] = jnp.transpose(flat[...])
    width = down_weight.shape[1]
    for k in range(8):
        down_wide[:, k * width : (k + 1) * width] = jnp.transpose(down_weight[k])


def fine_kernel(first, group, parents, columns, pre_grad, down_wide, *refs):
    fine = refs[-1]
    rows, width = fine.shape[0] * parents // pre_grad.shape[0], fine.shape[1]
    grads = pre_grad[first * parents : (first + group) * parents, :]
    slot_grads = jnp.dot(grads, down_wide[...], preferred_element_type=F32).astype(BF16)
    for i in range(group):
        slots = lax.broadcasted_iota(jnp.int32, (rows, parents * 8), 1)
        place = columns[:rows, first + i : first + i + 1]
        chooser = jnp.where(slots == place, 1.0, 0.0).astype(BF16)
        tall = jnp.concatenate(
            [
                slot_grads[i * parents : (i + 1) * parents, k * width : (k + 1) * width]
                for k in range(8)
            ],
            axis=0,
        )
        fine[(first + i) * rows : (first + i + 1) * rows, :] = jnp.dot(
            chooser, tall, preferred_element_type=F32
        ).astype(BF16)


def tree(values):
    while len(values) > 1:
        values = [values[i] + values[i + 1] for i in range(0, len(values), 2)]
    return values[0]


def up_end_kernel(scale, ids, *refs):
    *pieces, up_grad = refs
    for i, piece in enumerate(pieces):
        up_grad[ids[0] ^ i] = piece[...].astype(F32) * scale


def down_end_kernel(scale, ids, *refs):
    *pieces, down_grad, bias_grad = refs
    rows, out_width = down_grad.shape[1:]
    width = pieces[0].shape[1]
    for i, piece in enumerate(pieces):
        m = ids[0] ^ i
        parts = out_width // width
        for j in range(parts):
            tile = piece[j * rows : (j + 1) * rows, :].astype(F32)
            down_grad[m, :, j * width : (j + 1) * width] = tile * scale

        @pl.when(m == 0)
        def _():
            lines = piece[parts * rows :, :].astype(F32)
            for j in range(parts):
                pair = lines[j : j + 1] + lines[parts + j : parts + j + 1]
                bias_grad[:, j * width : (j + 1) * width] = pair * scale


def finish(kernel, ids, pieces, shapes):
    vmem = pl.BlockSpec(memory_space=pltpu.VMEM)
    return pl.pallas_call(
        kernel,
        grid_spec=pltpu.PrefetchScalarGridSpec(
            num_scalar_prefetch=1,
            grid=(1,),
            in_specs=[vmem] * len(pieces),
            out_specs=[whole_spec(shape) for shape in shapes],
        ),
        out_shape=[jax.ShapeDtypeStruct(shape, F32) for shape in shapes],
        compiler_params=grant(12),
    )(ids, *pieces)


def grant(mebibytes):
    return pltpu.CompilerParams(vmem_limit_bytes=mebibytes << 20)


def whole_spec(shape):
    return pl.BlockSpec(shape, lambda *_: (0,) * len(shape))


def row_of(array, index):
    start = (index,) + (jnp.uint32(0),) * (array.ndim - 1)
    return lax.dynamic_slice(array, start, (1,) + array.shape[1:])[0]


def sum_plane(peers, mine, other):
    chips = mine.shape[0]
    arrived = swap(other, "scene", 1)

    def both(peer):
        return row_of(mine, peer) + row_of(arrived, peer).astype(F32)

    sends = {d: both(peers[d]).astype(BF16) for d in range(1, chips)}
    parts = {d: swap(sends[d], "scene", 2 * d) for d in far_first(chips)}
    return tree([both(peers[0])] + [parts[d].astype(F32) for d in range(1, chips)]).astype(BF16)


def far_first(count):
    return sorted(range(1, count), key=lambda d: -bin(d).count("1"))


def crop_order(count):
    return [2, 3, 1] if count == 4 else far_first(count)


def sum_crops(part):
    crops = lax.axis_size("crop")
    parts = {d: swap(part, "crop", d) for d in crop_order(crops)}
    return tree([part.astype(F32)] + [parts[d].astype(F32) for d in range(1, crops)]).astype(BF16)


def spread(done):
    chips = lax.axis_size("scene") // 2
    even = {d: swap(done, "scene", 2 * d) for d in far_first(chips)}
    even[0] = done
    odd = {d: swap(even[d], "scene", 1) for d in range(chips)}
    return [x for d in range(chips) for x in (even[d], odd[d])]


def cut(array, ids, distances):
    def kernel(ids, array, *refs):
        *parts, sems = refs
        copies = [
            pltpu.make_async_copy(array.at[ids[0] ^ k], part, sems.at[i])
            for i, (k, part) in enumerate(zip(distances, parts))
        ]
        for copy in copies:
            copy.start()
        for copy in copies:
            copy.wait()

    return pl.pallas_call(
        kernel,
        in_specs=[
            pl.BlockSpec(memory_space=pltpu.SMEM),
            pl.BlockSpec(memory_space=pltpu.HBM),
        ],
        out_specs=[pl.BlockSpec(memory_space=pltpu.VMEM)] * len(distances),
        out_shape=[pltpu.VMEM(array.shape[1:], array.dtype)] * len(distances),
        scratch_shapes=[pltpu.SemaphoreType.DMA((len(distances),))],
        compiler_params=grant(12),
    )(ids, pltpu.with_memory_space_constraint(array, pltpu.HBM))


def exchange(array, ids, groups):
    out = {}
    for group in groups:
        for k, part in zip(group, cut(array, ids, group)):
            out[k] = part if k == 0 else swap(part, "scene", k)
    return [out[k] for k in range(array.shape[0])]


def held_back(count):
    return HELD_BACK if count == 8 else [count - 1]


def exchange_order(count):
    return [2, 4, 6, 3, 5, 7, 1] if count == 8 else list(range(1, count))


def on_device(
    fine_feats,
    out_grad,
    pre_act,
    deep_grad,
    down_weight,
    up_weight,
    block_owner,
    parent_slot,
    child_offset,
):
    scene_count = lax.axis_size("scene")
    crop_count = lax.axis_size("crop")
    width = fine_feats.shape[2]
    out_width = pre_act.shape[5]
    capacity = pre_act.shape[3]
    parents = pre_act.shape[4]
    owners = block_owner[0, :, 0]
    blocks = owners.shape[0]
    fine_rows = fine_feats.shape[1]
    rows = fine_rows // blocks
    group = 256 // parents
    steps = blocks // group
    slots = group * parents
    me = lax.axis_index("scene").astype(jnp.uint32)
    chip_peers = [(me >> 1) ^ jnp.uint32(k) for k in range(scene_count // 2)]
    whole_me = me.astype(jnp.int32)
    ids = jnp.stack([whole_me, whole_me & 1])
    ids, chip_peers = lax.optimization_barrier((ids, chip_peers))
    order = exchange_order(scene_count)
    pre_received = exchange(pre_act[0, 0], ids, [order[:2], order[2:] + [0]])

    earlier = jnp.arange(blocks)[None, :] < jnp.arange(blocks)[:, None]
    same_owner = owners[:, None] == owners[None, :]
    slot_rank = jnp.sum(same_owner & earlier, axis=1).astype(jnp.int32)
    distance = owners ^ whole_me
    target = distance * capacity + slot_rank
    hit = target[None, :] == jnp.arange(scene_count * capacity, dtype=jnp.int32)[:, None]
    table = jnp.max(jnp.where(hit, jnp.arange(blocks, dtype=jnp.int32)[None, :], -1), axis=1)
    counts = jnp.sum(
        distance[None, :] == jnp.arange(scene_count, dtype=jnp.int32)[:, None], axis=1
    ).astype(jnp.int32)
    table = jnp.concatenate([table, counts])

    ids, table, chip_peers = lax.optimization_barrier((ids, table, chip_peers))
    lanes = -(-rows // 128) * 128
    vmem = pl.BlockSpec(memory_space=pltpu.VMEM)
    places, columns, down_wide = pl.pallas_call(
        lambda *refs: prepare_kernel(parents, *refs),
        in_specs=[vmem] * 3,
        out_specs=[vmem] * 3,
        out_shape=[
            jax.ShapeDtypeStruct((steps, group, rows), jnp.int32),
            pltpu.VMEM((lanes, blocks), jnp.int32),
            pltpu.VMEM((out_width, 8 * width), BF16),
        ],
        scratch_shapes=[pltpu.VMEM((blocks, lanes), jnp.int32)],
        compiler_params=grant(12),
    )(parent_slot, child_offset, down_weight)
    place_spec = pl.BlockSpec((1, group, rows), lambda g, *_: (g, 0, 0))
    fine_spec = pl.BlockSpec((group * rows, width), lambda g, *_: (g, 0))
    coarse_spec = pl.BlockSpec((slots, out_width), lambda g, *_: (g, 0))
    total_rows = blocks * parents
    coarse_f32 = pltpu.VMEM((total_rows, out_width), F32)

    hbm = pl.BlockSpec(memory_space=pltpu.HBM)
    smem = pl.BlockSpec(memory_space=pltpu.SMEM)
    feat_slots, cot_slots, conv = pl.pallas_call(
        expand_kernel,
        grid=(steps,),
        in_specs=[place_spec, fine_spec, fine_spec, whole_spec(up_weight.shape)],
        out_specs=[vmem] * 3,
        out_shape=[
            pltpu.VMEM((8 * width, total_rows), BF16),
            pltpu.VMEM((total_rows, 8 * width), BF16),
            coarse_f32,
        ],
        scratch_shapes=[
            pltpu.VMEM((out_width, 8 * width), BF16),
            pltpu.VMEM((slots, 8 * width), BF16),
        ],
        compiler_params=grant(12),
    )(
        places,
        pltpu.with_memory_space_constraint(fine_feats[0], pltpu.HBM),
        pltpu.with_memory_space_constraint(out_grad[0], pltpu.HBM),
        up_weight,
    )
    deep_whole, conv = lax.optimization_barrier((deep_grad[0, 0], conv))
    deep_received = exchange(deep_whole, ids, [order + [0]])

    chips = scene_count // 2

    def dealt(rows, columns):
        shape = (chips, rows, columns)
        return [pltpu.VMEM(shape, F32), pltpu.VMEM(shape, BF16)]

    up_rows, down_rows = 8 * out_width // scene_count, 8 * width // scene_count
    slope, up_mine, up_other = pl.pallas_call(
        lambda *refs: act_kernel(scene_count, *refs),
        in_specs=[smem, smem] + [vmem] * (scene_count + 1),
        out_specs=[vmem] * 3,
        out_shape=[coarse_f32] + dealt(up_rows, width),
        scratch_shapes=[
            pltpu.VMEM((total_rows, out_width), BF16),
            pltpu.VMEM((out_width, 8 * width), F32),
        ],
        compiler_params=grant(12),
    )(table, ids, *pre_received, cot_slots)
    up_part = sum_plane(chip_peers, up_mine, up_other)
    late = held_back(scene_count)
    early = [k for k in range(scene_count) if k not in late]
    pre_grad_shape = pltpu.VMEM((total_rows, out_width), BF16)
    pre_half, bias_half = pl.pallas_call(
        lambda *refs: early_kernel(scene_count, early, *refs),
        in_specs=[smem] + [vmem] * (len(early) + 2),
        out_specs=[vmem] * 2,
        out_shape=[pre_grad_shape, pltpu.VMEM((8, out_width), F32)],
        compiler_params=grant(12),
    )(table, *[deep_received[k] for k in early], conv, slope)
    pre_half, bias_half, up_part = lax.optimization_barrier((pre_half, bias_half, up_part))
    up_done = sum_crops(up_part)

    mine_shape, other_shape = dealt(
        out_width // width * down_rows + BIAS_ROWS, width
    )
    pre_grad, down_other, extra = pl.pallas_call(
        lambda *refs: pre_kernel(scene_count, late, *refs),
        in_specs=[smem, smem] + [vmem] * (len(late) + 5),
        out_specs=[vmem] * 3,
        out_shape=[pre_grad_shape, other_shape, pltpu.VMEM((BIAS_ROWS, width), F32)],
        scratch_shapes=[pltpu.VMEM((8, out_width), F32)],
        input_output_aliases={len(late) + 5: 0},
        compiler_params=grant(12),
    )(table, ids, *[deep_received[k] for k in late], feat_slots, conv, slope, pre_half, bias_half)
    down_mine = pl.pallas_call(
        own_kernel,
        in_specs=[smem] + [vmem] * 3,
        out_specs=vmem,
        out_shape=mine_shape,
        compiler_params=grant(12),
    )(ids, feat_slots, pre_grad, extra)
    down_part = sum_plane(chip_peers, down_mine, down_other)
    down_done = sum_crops(down_part)
    down_pieces = spread(down_done)
    up_pieces = spread(up_done)

    fine = None
    first = 0
    for part, share in enumerate(FINE_SHARES):
        group = blocks * share // sum(FINE_SHARES)
        held = [] if part == 0 else [fine]
        fine = pl.pallas_call(
            lambda *refs, first=first, group=group: fine_kernel(first, group, parents, *refs),
            in_specs=[vmem] * (3 + len(held)),
            out_specs=vmem,
            out_shape=pltpu.VMEM((fine_rows, width), BF16),
            input_output_aliases={3: 0} if held else {},
            compiler_params=grant(12),
        )(columns, pre_grad, down_wide, *held)
        first += group

    scale = float(crop_count * scene_count * fine_rows) ** (-0.5)
    (up_grad,) = finish(
        lambda *refs: up_end_kernel(scale, *refs),
        ids,
        up_pieces,
        [(scene_count, up_rows, width)],
    )
    down_grad, bias_grad = finish(
        lambda *refs: down_end_kernel(scale, *refs),
        ids,
        down_pieces,
        [(scene_count, down_rows, out_width), (1, out_width)],
    )
    return (
        fine[None],
        down_grad.reshape(8, width, out_width),
        up_grad.reshape(8, out_width, width),
        bias_grad.reshape(out_width),
    )


def solution(mesh):
    return jax.shard_map(
        on_device,
        mesh=mesh,
        in_specs=(
            P("crop", "scene", None),
            P("crop", "scene", None),
            P("crop", "scene", None, None, None, None),
            P("crop", "scene", None, None, None, None),
            P(),
            P(),
            P("crop", "scene", None),
            P("crop", "scene"),
            P("crop", "scene"),
        ),
        out_specs=(P("crop", "scene", None), P(), P(), P()),
        check_vma=False,
    )
```

```python
import jax
import jax.numpy as jnp
from jax import lax
from jax.experimental import pallas as pl
from jax.experimental.pallas import tpu as pltpu
from jax.sharding import PartitionSpec as P


F32 = jnp.float32
BF16 = jnp.bfloat16
NT = (((1,), (1,)), ((), ()))
TN = (((0,), (0,)), ((), ()))
BIAS_ROWS = 8
FINE_SHARES = (16, 12, 4)
HELD_BACK = [7, 5]


def swap(value, axis, step):
    size = lax.axis_size(axis)
    return lax.ppermute(value, axis, [(i, i ^ step) for i in range(size)])


def expand_kernel(places, feats, cotan, up_weight, feat_slots, cot_slots, conv, wide, slot_rows):
    step = pl.program_id(0)
    group = places.shape[1]
    rows, width = feats.shape[0] // group, feats.shape[1]
    parents = slot_rows.shape[0] // group
    slots = slot_rows.shape[0]

    @pl.when(step == 0)
    def _():
        for k in range(8):
            wide[:, k * width : (k + 1) * width] = up_weight[k]

    at = pl.ds(pl.multiple_of(step * slots, slots), slots)
    for i in range(group):
        place = places[0, i : i + 1, :]
        ids = lax.broadcasted_iota(jnp.int32, (parents * 8, rows), 0)
        chooser = jnp.where(ids == place, 1.0, 0.0).astype(BF16)
        both = jnp.concatenate(
            [feats[i * rows : (i + 1) * rows, :], cotan[i * rows : (i + 1) * rows, :]], axis=1
        )
        spread = jnp.dot(chooser, both, preferred_element_type=F32).astype(BF16)
        for k in range(8):
            to = (slice(i * parents, (i + 1) * parents), slice(k * width, (k + 1) * width))
            slot_rows[to] = spread[k * parents : (k + 1) * parents, :width]
            cot_slots[
                pl.ds(pl.multiple_of(step * slots + i * parents, parents), parents),
                k * width : (k + 1) * width,
            ] = spread[k * parents : (k + 1) * parents, width:]
    feat_slots[:, at] = jnp.transpose(slot_rows[...])
    conv[at, :] = lax.dot_general(cot_slots[at, :], wide[...], NT, preferred_element_type=F32)


def each_block(table, count, received, body):
    for k, ref in received.items():
        capacity = ref.shape[0]

        def one(j, _, k=k, ref=ref, capacity=capacity):
            body(ref, j, table[k * capacity + j])

        lax.fori_loop(0, table[count * capacity + k], one, None)


def scene_here():
    return lax.axis_index("scene").astype(jnp.int32)


def deal(tiles, mine, other):
    core = scene_here() % 2
    for m, tile in enumerate(tiles):

        @pl.when(core == m % 2)
        def _():
            mine[m // 2] = tile

        @pl.when(core != m % 2)
        def _():
            other[m // 2] = tile.astype(BF16)


def act_kernel(count, table, *refs):
    received, (cot_slots, slope, mine, other, act, total) = refs[:count], refs[count:]
    parents = received[0].shape[1]

    def silu(ref, j, block):
        pre = ref[j].astype(F32)
        sig = 0.5 * jnp.tanh(0.5 * pre) + 0.5
        at = pl.ds(pl.multiple_of(block * parents, parents), parents)
        slope[at, :] = sig * (1.0 + pre * (1.0 - sig))
        act[at, :] = (pre * sig).astype(BF16)

    each_block(table, count, dict(enumerate(received)), silu)
    total[...] = lax.dot_general(act[...], cot_slots[...], TN, preferred_element_type=F32)
    pieces, rows, width = 2 * mine.shape[0], mine.shape[1], mine.shape[2]
    per = pieces // 8
    tiles = [
        total[(m % per) * rows : (m % per + 1) * rows, m // per * width : (m // per + 1) * width]
        for m in range(pieces)
    ]
    deal(tiles, mine, other)


def grad_blocks(table, count, received, conv, slope, pre_grad, bias):
    def one(ref, j, block):
        parents = ref.shape[1]
        at = pl.ds(pl.multiple_of(block * parents, parents), parents)
        grad = ((ref[j].astype(F32) + conv[at, :]) * slope[at, :]).astype(BF16)
        pre_grad[at, :] = grad
        wide = grad.astype(F32)
        bias[...] += jnp.sum(wide.reshape(-1, 8, wide.shape[1]), axis=0)

    each_block(table, count, received, one)


def early_kernel(count, distances, table, *refs):
    *received, conv, slope, pre_grad, bias = refs
    bias[...] = jnp.zeros_like(bias)
    grad_blocks(table, count, dict(zip(distances, received)), conv, slope, pre_grad, bias)


def pre_kernel(count, distances, table, *refs):
    received, rest = refs[: len(distances)], refs[len(distances) :]
    feat_slots, conv, slope, _, half_bias, pre_grad, other, extra, bias = rest
    bias[...] = half_bias[...]
    grad_blocks(table, count, dict(zip(distances, received)), conv, slope, pre_grad, bias)
    line = jnp.sum(bias[...], axis=0, keepdims=True)
    high = line.astype(BF16).astype(F32)
    width = extra.shape[1]
    extra[...] = jnp.zeros_like(extra)
    for i, part in enumerate((high, line - high)):
        for j in range(line.shape[1] // width):
            at = i * (line.shape[1] // width) + j
            extra[at : at + 1, :] = part[:, j * width : (j + 1) * width]
    down_pieces(1 - scene_here() % 2, feat_slots, pre_grad, extra, other)


def own_kernel(feat_slots, pre_grad, extra, mine):
    down_pieces(scene_here() % 2, feat_slots, pre_grad, extra, mine)


def down_pieces(core, feat_slots, pre_grad, extra, out):
    chips, _, width = out.shape
    rows = feat_slots.shape[0] // (2 * chips)
    lines = [
        feat_slots[pl.ds(pl.multiple_of((2 * i + core) * rows, rows), rows), :]
        for i in range(chips)
    ]
    total = jnp.dot(jnp.concatenate(lines, axis=0), pre_grad[...], preferred_element_type=F32)
    for i in range(chips):
        for j in range(total.shape[1] // width):
            tile = total[i * rows : (i + 1) * rows, j * width : (j + 1) * width]
            out[i, j * rows : (j + 1) * rows, :] = tile.astype(out.dtype)
        out[i, out.shape[1] - BIAS_ROWS :, :] = extra[...].astype(out.dtype)


def prepare_kernel(
    parents, parent_slot, child_offset, down_weight, places, columns, down_wide, flat
):
    steps, group, rows = places.shape
    flat[...] = jnp.zeros_like(flat)
    for block in range(steps * group):
        at = slice(block * rows, (block + 1) * rows)
        place = child_offset[0:1, at] * parents + parent_slot[0:1, at]
        places[block // group, block % group : block % group + 1, :] = place
        flat[block : block + 1, :rows] = place
    columns[...] = jnp.transpose(flat[...])
    width = down_weight.shape[1]
    for k in range(8):
        down_wide[:, k * width : (k + 1) * width] = jnp.transpose(down_weight[k])


def fine_kernel(first, group, parents, columns, pre_grad, down_wide, *refs):
    fine = refs[-1]
    rows, width = fine.shape[0] * parents // pre_grad.shape[0], fine.shape[1]
    grads = pre_grad[first * parents : (first + group) * parents, :]
    slot_grads = jnp.dot(grads, down_wide[...], preferred_element_type=F32).astype(BF16)
    for i in range(group):
        slots = lax.broadcasted_iota(jnp.int32, (rows, parents * 8), 1)
        place = columns[:rows, first + i : first + i + 1]
        chooser = jnp.where(slots == place, 1.0, 0.0).astype(BF16)
        tall = jnp.concatenate(
            [
                slot_grads[i * parents : (i + 1) * parents, k * width : (k + 1) * width]
                for k in range(8)
            ],
            axis=0,
        )
        fine[(first + i) * rows : (first + i + 1) * rows, :] = jnp.dot(
            chooser, tall, preferred_element_type=F32
        ).astype(BF16)


def tree(values):
    while len(values) > 1:
        values = [values[i] + values[i + 1] for i in range(0, len(values), 2)]
    return values[0]


def up_end_kernel(scale, *refs):
    *pieces, up_grad = refs
    me = scene_here()
    for i, piece in enumerate(pieces):
        up_grad[me ^ i] = piece[...].astype(F32) * scale


def down_end_kernel(scale, *refs):
    me = scene_here()
    *pieces, down_grad, bias_grad = refs
    rows, out_width = down_grad.shape[1:]
    width = pieces[0].shape[1]
    for i, piece in enumerate(pieces):
        m = me ^ i
        parts = out_width // width
        for j in range(parts):
            tile = piece[j * rows : (j + 1) * rows, :].astype(F32)
            down_grad[m, :, j * width : (j + 1) * width] = tile * scale

        @pl.when(m == 0)
        def _():
            lines = piece[parts * rows :, :].astype(F32)
            for j in range(parts):
                pair = lines[j : j + 1] + lines[parts + j : parts + j + 1]
                bias_grad[:, j * width : (j + 1) * width] = pair * scale


def finish(kernel, pieces, shapes):
    vmem = pl.BlockSpec(memory_space=pltpu.VMEM)
    return pl.pallas_call(
        kernel,
        grid=(1,),
        in_specs=[vmem] * len(pieces),
        out_specs=[whole_spec(shape) for shape in shapes],
        out_shape=[jax.ShapeDtypeStruct(shape, F32) for shape in shapes],
        compiler_params=grant(12),
    )(*pieces)


def grant(mebibytes):
    return pltpu.CompilerParams(vmem_limit_bytes=mebibytes << 20)


def whole_spec(shape):
    return pl.BlockSpec(shape, lambda *_: (0,) * len(shape))


def row_of(array, index):
    start = (index,) + (jnp.uint32(0),) * (array.ndim - 1)
    return lax.dynamic_slice(array, start, (1,) + array.shape[1:])[0]


def sum_plane(peers, mine, other):
    chips = mine.shape[0]
    arrived = swap(other, "scene", 1)

    def both(peer):
        return row_of(mine, peer) + row_of(arrived, peer).astype(F32)

    sends = {d: both(peers[d]).astype(BF16) for d in range(1, chips)}
    parts = {d: swap(sends[d], "scene", 2 * d) for d in far_first(chips)}
    return tree([both(peers[0])] + [parts[d].astype(F32) for d in range(1, chips)]).astype(BF16)


def far_first(count):
    return sorted(range(1, count), key=lambda d: -bin(d).count("1"))


def crop_order(count):
    return [2, 3, 1] if count == 4 else far_first(count)


def sum_crops(part):
    crops = lax.axis_size("crop")
    parts = {d: swap(part, "crop", d) for d in crop_order(crops)}
    return tree([part.astype(F32)] + [parts[d].astype(F32) for d in range(1, crops)]).astype(BF16)


def spread(done):
    chips = lax.axis_size("scene") // 2
    even = {d: swap(done, "scene", 2 * d) for d in far_first(chips)}
    even[0] = done
    odd = {d: swap(even[d], "scene", 1) for d in range(chips)}
    return [x for d in range(chips) for x in (even[d], odd[d])]


def cut(array, distances):
    def kernel(array, *refs):
        *parts, sems = refs
        me = scene_here()
        copies = [
            pltpu.make_async_copy(array.at[me ^ k], part, sems.at[i])
            for i, (k, part) in enumerate(zip(distances, parts))
        ]
        for copy in copies:
            copy.start()
        for copy in copies:
            copy.wait()

    return pl.pallas_call(
        kernel,
        in_specs=[pl.BlockSpec(memory_space=pltpu.HBM)],
        out_specs=[pl.BlockSpec(memory_space=pltpu.VMEM)] * len(distances),
        out_shape=[pltpu.VMEM(array.shape[1:], array.dtype)] * len(distances),
        scratch_shapes=[pltpu.SemaphoreType.DMA((len(distances),))],
        compiler_params=grant(12),
    )(pltpu.with_memory_space_constraint(array, pltpu.HBM))


def exchange(array, groups):
    out = {}
    for group in groups:
        for k, part in zip(group, cut(array, group)):
            out[k] = part if k == 0 else swap(part, "scene", k)
    return [out[k] for k in range(array.shape[0])]


def held_back(count):
    return HELD_BACK if count == 8 else [count - 1]


def exchange_order(count):
    return [2, 4, 6, 3, 5, 7, 1] if count == 8 else list(range(1, count))


def on_device(
    fine_feats,
    out_grad,
    pre_act,
    deep_grad,
    down_weight,
    up_weight,
    block_owner,
    parent_slot,
    child_offset,
):
    scene_count = lax.axis_size("scene")
    crop_count = lax.axis_size("crop")
    width = fine_feats.shape[2]
    out_width = pre_act.shape[5]
    capacity = pre_act.shape[3]
    parents = pre_act.shape[4]
    owners = block_owner[0, :, 0]
    blocks = owners.shape[0]
    fine_rows = fine_feats.shape[1]
    rows = fine_rows // blocks
    group = 256 // parents
    steps = blocks // group
    slots = group * parents
    me = lax.axis_index("scene").astype(jnp.uint32)
    chip_peers = [(me >> 1) ^ jnp.uint32(k) for k in range(scene_count // 2)]
    whole_me = me.astype(jnp.int32)
    pre_whole, whole_me, chip_peers = lax.optimization_barrier(
        (pre_act[0, 0], whole_me, chip_peers)
    )
    order = exchange_order(scene_count)
    pre_received = exchange(pre_whole, [order[:2], order[2:] + [0]])

    earlier = jnp.arange(blocks)[None, :] < jnp.arange(blocks)[:, None]
    same_owner = owners[:, None] == owners[None, :]
    slot_rank = jnp.sum(same_owner & earlier, axis=1).astype(jnp.int32)
    distance = owners ^ whole_me
    target = distance * capacity + slot_rank
    hit = target[None, :] == jnp.arange(scene_count * capacity, dtype=jnp.int32)[:, None]
    table = jnp.max(jnp.where(hit, jnp.arange(blocks, dtype=jnp.int32)[None, :], -1), axis=1)
    counts = jnp.sum(
        distance[None, :] == jnp.arange(scene_count, dtype=jnp.int32)[:, None], axis=1
    ).astype(jnp.int32)
    table = jnp.concatenate([table, counts])

    table, chip_peers = lax.optimization_barrier((table, chip_peers))
    lanes = -(-rows // 128) * 128
    vmem = pl.BlockSpec(memory_space=pltpu.VMEM)
    places, columns, down_wide = pl.pallas_call(
        lambda *refs: prepare_kernel(parents, *refs),
        in_specs=[vmem] * 3,
        out_specs=[vmem] * 3,
        out_shape=[
            jax.ShapeDtypeStruct((steps, group, rows), jnp.int32),
            pltpu.VMEM((lanes, blocks), jnp.int32),
            pltpu.VMEM((out_width, 8 * width), BF16),
        ],
        scratch_shapes=[pltpu.VMEM((blocks, lanes), jnp.int32)],
        compiler_params=grant(12),
    )(parent_slot, child_offset, down_weight)
    place_spec = pl.BlockSpec((1, group, rows), lambda g, *_: (g, 0, 0))
    fine_spec = pl.BlockSpec((group * rows, width), lambda g, *_: (g, 0))
    coarse_spec = pl.BlockSpec((slots, out_width), lambda g, *_: (g, 0))
    total_rows = blocks * parents
    coarse_f32 = pltpu.VMEM((total_rows, out_width), F32)

    hbm = pl.BlockSpec(memory_space=pltpu.HBM)
    smem = pl.BlockSpec(memory_space=pltpu.SMEM)
    feat_slots, cot_slots, conv = pl.pallas_call(
        expand_kernel,
        grid=(steps,),
        in_specs=[place_spec, fine_spec, fine_spec, whole_spec(up_weight.shape)],
        out_specs=[vmem] * 3,
        out_shape=[
            pltpu.VMEM((8 * width, total_rows), BF16),
            pltpu.VMEM((total_rows, 8 * width), BF16),
            coarse_f32,
        ],
        scratch_shapes=[
            pltpu.VMEM((out_width, 8 * width), BF16),
            pltpu.VMEM((slots, 8 * width), BF16),
        ],
        compiler_params=grant(12),
    )(
        places,
        pltpu.with_memory_space_constraint(fine_feats[0], pltpu.HBM),
        pltpu.with_memory_space_constraint(out_grad[0], pltpu.HBM),
        up_weight,
    )
    deep_whole, conv = lax.optimization_barrier((deep_grad[0, 0], conv))
    deep_received = exchange(deep_whole, [order + [0]])

    chips = scene_count // 2

    def dealt(rows, columns):
        shape = (chips, rows, columns)
        return [pltpu.VMEM(shape, F32), pltpu.VMEM(shape, BF16)]

    up_rows, down_rows = 8 * out_width // scene_count, 8 * width // scene_count
    slope, up_mine, up_other = pl.pallas_call(
        lambda *refs: act_kernel(scene_count, *refs),
        in_specs=[smem] + [vmem] * (scene_count + 1),
        out_specs=[vmem] * 3,
        out_shape=[coarse_f32] + dealt(up_rows, width),
        scratch_shapes=[
            pltpu.VMEM((total_rows, out_width), BF16),
            pltpu.VMEM((out_width, 8 * width), F32),
        ],
        compiler_params=grant(12),
    )(table, *pre_received, cot_slots)
    up_part = sum_plane(chip_peers, up_mine, up_other)
    late = held_back(scene_count)
    early = [k for k in range(scene_count) if k not in late]
    pre_grad_shape = pltpu.VMEM((total_rows, out_width), BF16)
    pre_half, bias_half = pl.pallas_call(
        lambda *refs: early_kernel(scene_count, early, *refs),
        in_specs=[smem] + [vmem] * (len(early) + 2),
        out_specs=[vmem] * 2,
        out_shape=[pre_grad_shape, pltpu.VMEM((8, out_width), F32)],
        compiler_params=grant(12),
    )(table, *[deep_received[k] for k in early], conv, slope)
    pre_half, bias_half, up_part = lax.optimization_barrier((pre_half, bias_half, up_part))
    up_done = sum_crops(up_part)

    mine_shape, other_shape = dealt(
        out_width // width * down_rows + BIAS_ROWS, width
    )
    pre_grad, down_other, extra = pl.pallas_call(
        lambda *refs: pre_kernel(scene_count, late, *refs),
        in_specs=[smem] + [vmem] * (len(late) + 5),
        out_specs=[vmem] * 3,
        out_shape=[pre_grad_shape, other_shape, pltpu.VMEM((BIAS_ROWS, width), F32)],
        scratch_shapes=[pltpu.VMEM((8, out_width), F32)],
        input_output_aliases={len(late) + 4: 0},
        compiler_params=grant(12),
    )(
        table,
        *[deep_received[k] for k in late],
        feat_slots,
        conv,
        slope,
        pre_half,
        bias_half,
    )
    down_mine = pl.pallas_call(
        own_kernel,
        in_specs=[vmem] * 3,
        out_specs=vmem,
        out_shape=mine_shape,
        compiler_params=grant(12),
    )(feat_slots, pre_grad, extra)
    down_part = sum_plane(chip_peers, down_mine, down_other)
    down_done = sum_crops(down_part)
    down_pieces = spread(down_done)
    up_pieces = spread(up_done)

    fine = None
    first = 0
    for part, share in enumerate(FINE_SHARES):
        group = blocks * share // sum(FINE_SHARES)
        held = [] if part == 0 else [fine]
        fine = pl.pallas_call(
            lambda *refs, first=first, group=group: fine_kernel(first, group, parents, *refs),
            in_specs=[vmem] * (3 + len(held)),
            out_specs=vmem,
            out_shape=pltpu.VMEM((fine_rows, width), BF16),
            input_output_aliases={3: 0} if held else {},
            compiler_params=grant(12),
        )(columns, pre_grad, down_wide, *held)
        first += group

    scale = float(crop_count * scene_count * fine_rows) ** (-0.5)
    (up_grad,) = finish(
        lambda *refs: up_end_kernel(scale, *refs),
        up_pieces,
        [(scene_count, up_rows, width)],
    )
    down_grad, bias_grad = finish(
        lambda *refs: down_end_kernel(scale, *refs),
        down_pieces,
        [(scene_count, down_rows, out_width), (1, out_width)],
    )
    return (
        fine[None],
        down_grad.reshape(8, width, out_width),
        up_grad.reshape(8, out_width, width),
        bias_grad.reshape(out_width),
    )


def solution(mesh):
    return jax.shard_map(
        on_device,
        mesh=mesh,
        in_specs=(
            P("crop", "scene", None),
            P("crop", "scene", None),
            P("crop", "scene", None, None, None, None),
            P("crop", "scene", None, None, None, None),
            P(),
            P(),
            P("crop", "scene", None),
            P("crop", "scene"),
            P("crop", "scene"),
        ),
        out_specs=(P("crop", "scene", None), P(), P(), P()),
        check_vma=False,
    )
```
